512 devices in a mesh: gx: 32 (over z, core), gy: 16 (over y, x).
Axes of the slice: x: 4, y: 4, z: 16, core: 2. Of those that a mesh axis runs over, the one named last changes fastest.
Arguments:
- thermal_anomaly: float32 [16, 128, 4096], P(None, 'gy', 'gx'), may hold values from -6 to 6
- saltiness_anomaly: float32 [16, 128, 4096], P(None, 'gy', 'gx'), may hold values from -6 to 6
- zonal_volume_rate: float32 [16, 128, 4096], P(None, 'gy', 'gx'), may hold values from -0.12 to 0.12
- meridional_volume_rate: float32 [16, 128, 4096], P(None, 'gy', 'gx'), may hold values from -0.12 to 0.12
- sideways_diffusivity_factor: float32 [128, 4096], P('gy', 'gx'), may hold values from 0.02 to 0.13
- stratum_interface_mixing: float32 [15, 128, 4096], P(None, 'gy', 'gx'), may hold values from 0.05 to 20
- flooded_strata: int32 [128, 4096], P('gy', 'gx'), may hold values from 0 to 16
- patch_sea_source: int32 [16, 65536], P('gy', 'gx'), may hold values from 0 to 1023, as said below
- patch_sky_target: int32 [16, 65536], P('gy', 'gx'), may hold values from 0 to 8191, as said below
- patch_measure_pointer: int32 [16, 65536], P('gy', 'gx'), may hold values from 0 to 63
- patch_measures: float32 [64], replicated, may hold values from 0.05 to 1
- holder_ordering: int32 [16, 8192], P('gy'), may hold values from 0 to 8191, as said below
Outputs:
- temperature_next: float32 [16, 128, 4096], P(None, 'gy', 'gx')
- salinity_next: float32 [16, 128, 4096], P(None, 'gy', 'gx')
- air_sums: float32 [2, 16, 8192], P(None, 'gy', 'gx')
The draws below stay inside these ranges and needn't reach their ends.
Inputs may be any that keep to these rules, and one draw needn't show every extreme that they name: `patch_sea_source`: Row-major index of the ocean cell within the 8 x 128 tile of the device that holds the entry. `patch_sky_target`: Row-major index over the atmosphere cells of the row of tiles, half of 8 rows by half of 4096 columns, each covering 2 x 2 ocean cells; it is the cell containing the intersection's ocean cell, its eastern neighbour (periodic), or its northern or southern neighbour within the row of tiles. `holder_ordering`: each row is a permutation. Call the atmosphere cells of columns q * 64 to (q + 1) * 64 - 1 of a row the cells over tile column q; for every q and every owner o (place // 256 = o), exactly 8 cells over tile column q have owner o.
All inputs are finite; a program needn't handle non-finite values.
Results may differ from the reference program's by a relative error of at most 0.00002.
Values sent between devices are 32-bit elements; how exact they have to be, the bound alone decides.
No kernel may reach another device: no remote copies, remote signals or barrier semaphores. Data moves between devices by JAX's collectives and lax.ppermute only.
A program may use at most 64 MiB of HBM per device.

```python
import math
import jax
import jax.numpy as jnp

CX = 128
CY = 8
STRATA_TOTAL = 16
NSUB = 4
NAREA = 64
TILE_COLS = 32
TILE_ROWS = 16
ZONAL_EXTENT = 4096
MERIDIONAL_SPAN = 128
NOV = 2048
NATM_ROW = 8192
N_GX = 32
N_GY = 16


def intersection_pair(key):
    tile_rows = MERIDIONAL_SPAN // CY
    tile_cols = ZONAL_EXTENT // CX
    total = tile_cols * NOV
    cells = jax.random.randint(jax.random.fold_in(key, 11), (tile_rows, total), 0, CY * CX)
    modes = jax.random.randint(jax.random.fold_in(key, 12), (tile_rows, total), 0, 3)
    entry = jnp.arange(total)[None, :] % NOV
    cells = jnp.where(entry == 0, CY * CX - 1, jnp.where(entry == 1, 0, cells))
    modes = jnp.where(entry < 2, 0, modes)
    column = jnp.arange(total)[None, :] // NOV
    air_row = cells // CX // 2
    air_col = (column * CX + cells % CX) // 2
    air_col = jnp.where(modes == 1, (air_col + 1) % (ZONAL_EXTENT // 2), air_col)
    air_row = jnp.where(modes == 2, jnp.where(air_row + 1 < CY // 2, air_row + 1, air_row - 1), air_row)
    target = air_row * (ZONAL_EXTENT // 2) + air_col
    return (cells.astype(jnp.int32), target.astype(jnp.int32))


def draw_patch_sea_source(key, part):
    return intersection_pair(key)[0]


def draw_patch_sky_target(key, part):
    return intersection_pair(key)[1]


def owner_row(row_key):
    tiles = ZONAL_EXTENT // CX
    air_height = CY // 2
    air_width = CX // 2
    owned = air_height * air_width
    per_owner = owned // tiles
    block_keys = jax.random.split(jax.random.fold_in(row_key, 1), tiles)
    shuffled = jax.vmap(lambda k: jax.random.permutation(k, owned))(block_keys)
    owner = shuffled % tiles
    ranks = shuffled // tiles
    owner_keys = jax.random.split(jax.random.fold_in(row_key, 2), tiles)
    slot_orders = jax.vmap(lambda k: jax.random.permutation(k, owned))(owner_keys)
    raw_slot = jnp.arange(tiles)[:, None] * per_owner + ranks
    slot = slot_orders[owner, raw_slot]
    place = owner * owned + slot
    place = place.reshape(tiles, air_height, air_width).transpose(1, 0, 2).reshape(-1)
    return place


def draw_holder_ordering(key, part):
    tile_rows = MERIDIONAL_SPAN // CY
    row_keys = jax.random.split(jax.random.fold_in(key, 21), tile_rows)
    return jax.vmap(owner_row)(row_keys).astype(jnp.int32)


def with_ends(values, own_key, low, high):
    longest = values.shape.index(max(values.shape))
    spots = []
    for shift in (0, 1):
        where = [jax.random.randint(jax.random.fold_in(own_key, axis), (), 0, length) for axis, length in enumerate(values.shape)]
        where[longest] = (where[longest] + shift) % values.shape[longest]
        spots.append(tuple(where))
    return values.at[spots[0]].set(low).at[spots[1]].set(high)


def shard_levels(key, extent, cuts, low, high):
    def one(dim, shards_of):
        heights = jax.random.uniform(jax.random.fold_in(jax.random.fold_in(key, 6), dim), (shards_of,), jnp.float32, low / len(cuts), high / len(cuts))
        return jnp.repeat(jnp.exp(heights), extent[dim] // shards_of).reshape((-1,) + (1,) * (len(extent) - dim - 1))

    gain = one(*cuts[0])
    for cut in cuts[1:]:
        gain = gain * one(*cut)
    return gain


def centred(own_key, dims, deviation, reach, shards=(), held_as=jnp.bfloat16):
    values = deviation * jax.random.normal(own_key, dims, jnp.float32)
    if shards:
        values = values * shard_levels(own_key, dims, shards, -0.22, 0.18)
    return jnp.clip(values, -reach, reach).astype(held_as)


def setup_inputs(seed: int = 0) -> dict:
    key_list = jax.random.split(jax.random.key(seed), 13)
    thermal_anomaly = centred(key_list[0], (STRATA_TOTAL, MERIDIONAL_SPAN, ZONAL_EXTENT), 1.0, 6.0, ((1, 16), (2, 32)), jnp.float32)
    saltiness_anomaly = centred(key_list[1], (STRATA_TOTAL, MERIDIONAL_SPAN, ZONAL_EXTENT), 1.0, 6.0, ((1, 16), (2, 32)), jnp.float32)
    zonal_volume_rate = jnp.clip(jax.random.uniform(key_list[2], (STRATA_TOTAL, MERIDIONAL_SPAN, ZONAL_EXTENT), jnp.float32, -0.12, 0.12) * shard_levels(key_list[2], (STRATA_TOTAL, MERIDIONAL_SPAN, ZONAL_EXTENT), ((1, 16), (2, 32)), -0.4, 0.0), -0.12, 0.12)
    meridional_volume_rate = jnp.clip(jax.random.uniform(key_list[3], (STRATA_TOTAL, MERIDIONAL_SPAN, ZONAL_EXTENT), jnp.float32, -0.12, 0.12) * shard_levels(key_list[3], (STRATA_TOTAL, MERIDIONAL_SPAN, ZONAL_EXTENT), ((1, 16), (2, 32)), -0.4, 0.0), -0.12, 0.12)
    sideways_diffusivity_factor = jnp.clip(jnp.exp(math.log(0.13) - 1.8718022 * jax.random.uniform(key_list[4], (MERIDIONAL_SPAN, ZONAL_EXTENT), jnp.float32) ** shard_levels(key_list[4], (MERIDIONAL_SPAN, ZONAL_EXTENT), ((0, 16), (1, 32)), -0.2, 0.2)), 0.02, 0.13)
    stratum_interface_mixing = jnp.clip(jnp.exp(math.log(20.0) - 5.9914645 * jax.random.uniform(key_list[5], (STRATA_TOTAL - 1, MERIDIONAL_SPAN, ZONAL_EXTENT), jnp.float32) ** shard_levels(key_list[5], (STRATA_TOTAL - 1, MERIDIONAL_SPAN, ZONAL_EXTENT), ((1, 16), (2, 32)), -0.2, 0.2)), 0.05, 20.0)
    flooded_strata = with_ends(jax.random.randint(key_list[6], (MERIDIONAL_SPAN, ZONAL_EXTENT), 0, STRATA_TOTAL + 1), jax.random.fold_in(key_list[6], 1), 0, STRATA_TOTAL).astype(jnp.int32)
    patch_sea_source = draw_patch_sea_source(jax.random.fold_in(key_list[12], 71), 0)
    patch_sky_target = draw_patch_sky_target(jax.random.fold_in(key_list[12], 71), 0)
    patch_measure_pointer = with_ends(jax.random.randint(key_list[9], (TILE_ROWS, TILE_COLS * NOV), 0, NAREA), jax.random.fold_in(key_list[9], 1), 0, NAREA - 1).astype(jnp.int32)
    patch_measures = jnp.clip(jnp.exp(jax.random.uniform(key_list[10], (NAREA,), jnp.float32, math.log(0.05), math.log(1.0))), 0.05, 1.0)
    holder_ordering = draw_holder_ordering(jax.random.fold_in(key_list[12], 71), 0)
    return dict(thermal_anomaly=thermal_anomaly, saltiness_anomaly=saltiness_anomaly, zonal_volume_rate=zonal_volume_rate, meridional_volume_rate=meridional_volume_rate, sideways_diffusivity_factor=sideways_diffusivity_factor, stratum_interface_mixing=stratum_interface_mixing, flooded_strata=flooded_strata, patch_sea_source=patch_sea_source, patch_sky_target=patch_sky_target, patch_measure_pointer=patch_measure_pointer, patch_measures=patch_measures, holder_ordering=holder_ordering)


def advance(quantity, east_vel, north_vel, diffusivity, wetness):
    open_east = wetness[:, :, :-1] * wetness[:, :, 1:]
    kappa_east = 0.5 * (diffusivity[:, :-1] + diffusivity[:, 1:])
    speed = east_vel[:, :, :-1]
    left = quantity[..., :-1]
    right = quantity[..., 1:]
    flux_east = open_east * (jnp.maximum(speed, 0.0) * left + jnp.minimum(speed, 0.0) * right - kappa_east * (right - left))
    open_north = wetness[:, :-1, :] * wetness[:, 1:, :]
    kappa_north = 0.5 * (diffusivity[:-1, :] + diffusivity[1:, :])
    northward = north_vel[:, :-1, :]
    lower = quantity[:, :, :-1, :]
    upper = quantity[:, :, 1:, :]
    flux_north = open_north * (jnp.maximum(northward, 0.0) * lower + jnp.minimum(northward, 0.0) * upper - kappa_north * (upper - lower))
    across = flux_east[..., 1:] - flux_east[..., :-1]
    along = flux_north[:, :, 1:, :] - flux_north[:, :, :-1, :]
    return quantity[:, :, 1:-1, 1:-1] - (across[:, :, 1:-1, :] + along[:, :, :, 1:-1])


def column_solve(quantity, vertical, wetness):
    coupling = vertical * wetness[:-1] * wetness[1:]
    strata_stack = quantity.shape[1]
    ratios = []
    partial_value = []
    for level in range(strata_stack):
        below = coupling[level] if level < strata_stack - 1 else 0.0
        above = coupling[level - 1] if level > 0 else 0.0
        diagonal = 1.0 + above + below
        if level == 0:
            denom = diagonal
            value = quantity[:, 0]
        else:
            denom = diagonal + above * ratios[-1]
            value = quantity[:, level] + above * partial_value[-1]
        ratios.append(-below / denom)
        partial_value.append(value / denom)
    result = [None] * strata_stack
    result[strata_stack - 1] = partial_value[strata_stack - 1]
    for level in range(strata_stack - 2, -1, -1):
        result[level] = partial_value[level] - ratios[level] * result[level + 1]
    return jnp.stack(result, axis=1)


def extend(array):
    wrapped = jnp.concatenate([array[..., -1:], array, array[..., :1]], axis=-1)
    widths = [(0, 0)] * (array.ndim - 2) + [(1, 1), (0, 0)]
    return jnp.pad(wrapped, widths)


def reference(thermal_anomaly, saltiness_anomaly, zonal_volume_rate, meridional_volume_rate, sideways_diffusivity_factor, stratum_interface_mixing, flooded_strata, patch_sea_source, patch_sky_target, patch_measure_pointer, patch_measures, holder_ordering):
    wetness = (jnp.arange(STRATA_TOTAL)[:, None, None] < flooded_strata[None]).astype(jnp.float32)
    quantity = jnp.stack([thermal_anomaly, saltiness_anomaly])
    east_ext = extend(zonal_volume_rate)
    north_ext = extend(meridional_volume_rate)
    kappa_ext = extend(sideways_diffusivity_factor)
    wet_ext = extend(wetness)
    for repeat in range(NSUB):
        quantity = advance(extend(quantity), east_ext, north_ext, kappa_ext, wet_ext)
    quantity = column_solve(quantity, stratum_interface_mixing, wetness)
    surface = quantity[:, 0]
    wet_top = wetness[0]
    tile_col = (jnp.arange(N_GX * NOV) // NOV)[None, :]
    tile_row = jnp.arange(N_GY)[:, None]
    grid_row = tile_row * CY + patch_sea_source // CX
    grid_col = tile_col * CX + patch_sea_source % CX
    weights = patch_measures[patch_measure_pointer] * wet_top[grid_row, grid_col]
    terms = surface[:, grid_row, grid_col] * weights[None]
    places = jnp.take_along_axis(holder_ordering, patch_sky_target, axis=1)
    flat = (tile_row * NATM_ROW + places).reshape(-1)
    summed = jax.ops.segment_sum(terms.reshape(2, -1).T, flat, num_segments=N_GY * NATM_ROW)
    air_sums = summed.T.reshape(2, N_GY, NATM_ROW)
    return quantity[0], quantity[1], air_sums
```

```python
import jax
import jax.numpy as jnp
from jax import lax
from jax.experimental import pallas as pl
from jax.experimental.pallas import tpu as pltpu
from jax.sharding import PartitionSpec as P

NSUB = 4
LEVELS = 16
ROWS = 8
LANES = 128
F32 = jnp.float32
BF16 = jnp.bfloat16


def iota(shape, dim):
    return lax.broadcasted_iota(jnp.int32, shape, dim)


def row_mask(parity):
    return (((iota((ROWS, LANES), 0) >> 2) + parity) & 1) == 0


def pack_kernel(t_ref, s_ref, u_ref, v_ref, kap_ref, dep_ref, col_ref, one_ref, two_ref):
    slot = iota((ROWS, LANES), 1) >> 3
    mask = row_mask(lax.axis_index("gy") & 1)
    for a, ref in enumerate((t_ref, s_ref, u_ref, v_ref)):
        strip = jnp.zeros((ROWS, LANES), F32)
        for k in range(LEVELS):
            strip = jnp.where(slot == k, pltpu.roll(ref[k], (8 * k + 4) % LANES, 1), strip)
        col_ref[a] = strip
        for k in range(8):
            here, there = ref[k], pltpu.roll(ref[k + 8], 4, 0)
            one_ref[a * 8 + k] = jnp.where(mask, there, here)
            two_ref[a * 8 + k] = jnp.where(mask, here, there)
    kap = kap_ref[...]
    dep = dep_ref[...].astype(F32)
    strip = jnp.where(slot == 0, pltpu.roll(kap, 4, 1), jnp.zeros((ROWS, LANES), F32))
    col_ref[4] = jnp.where(slot == 1, pltpu.roll(dep, 12, 1), strip)
    there = pltpu.roll(dep, 4, 0)
    one_ref[32] = jnp.where(mask, there, kap)
    two_ref[32] = jnp.where(mask, kap, there)


def side_columns(first_ref, second_ref):
    parity = lax.axis_index("gx") & 1
    mask = (((iota((ROWS, LANES), 1) >> 2) + parity) & 1) == 0
    return [jnp.where(mask, second_ref[a], first_ref[a]) for a in range(5)]


def corner_kernel(one_in, two_in, first_ref, second_ref, one_ref, two_ref):
    for i in range(33):
        one_ref[i] = one_in[i]
        two_ref[i] = two_in[i]
    side = side_columns(first_ref, second_ref)
    side.append(jnp.zeros((ROWS, LANES), F32))
    mask = row_mask(lax.axis_index("gy") & 1)
    for i in range(3):
        here, there = side[2 * i], pltpu.roll(side[2 * i + 1], 4, 0)
        one_ref[33 + i] = jnp.where(mask, there, here)
        two_ref[33 + i] = jnp.where(mask, here, there)


def prep_kernel(
    src_ref, sky_ref, ptr_ref, area_ref, place_ref, mix_ref, dep_ref,
    inv_ref, down_ref, up_ref, weight_ref, owner_ref, rank_ref, slot_ref,
):
    q = lax.axis_index("gx")
    dep = dep_ref[...]
    above = jnp.zeros((ROWS, LANES), F32)
    carry = jnp.zeros((ROWS, LANES), F32)
    for k in range(LEVELS):
        below = jnp.where(dep > k + 1, mix_ref[k], 0.0) if k < LEVELS - 1 else jnp.zeros((ROWS, LANES), F32)
        inv = 1.0 / ((1.0 + above + below) - above * carry)
        carry = below * inv
        inv_ref[k] = inv
        down_ref[k] = above * inv
        up_ref[k] = carry
        above = below
    src = src_ref[...]
    sky = sky_ref[...]
    row, col = src >> 7, src & 127
    table = area_ref[...]
    table = jnp.broadcast_to(jnp.concatenate([table, table], axis=1), (16, LANES))
    area = jnp.take_along_axis(table, ptr_ref[...], axis=1)
    rise = (sky >> 11) - (row >> 1)
    east = ((sky & 2047) - (q * 64 + (col >> 1))) & 2047
    kind = jnp.where(east == 1, 1, jnp.where(rise == 1, 2, jnp.where(rise == -1, 3, 0)))
    high = kind * 8 + row
    part = []
    rest = area
    for _ in range(3):
        piece = rest.astype(BF16).astype(F32)
        part.append(piece)
        rest = rest - piece
    sums = jnp.zeros((96, LANES), F32)
    for i in range(0, 16, 2):
        left, right = [], []
        for j in (i, i + 1):
            hit = jnp.broadcast_to(high[j : j + 1], (32, LANES)) == iota((32, LANES), 0)
            left.append(
                jnp.concatenate(
                    [jnp.where(hit, jnp.broadcast_to(p[j : j + 1], (32, LANES)), 0.0) for p in part], axis=0
                )
            )
            same = jnp.broadcast_to(col[j : j + 1], (LANES, LANES)) == iota((LANES, LANES), 0)
            right.append(jnp.where(same, 1.0, 0.0))
        sums = sums + lax.dot_general(
            jnp.concatenate(left, axis=1).astype(BF16),
            jnp.concatenate(right, axis=1).astype(BF16),
            (((1,), (1,)), ((), ())),
            preferred_element_type=F32,
        )
    sums = sums[0:32] + sums[32:64] + sums[64:96]
    wet = jnp.where(dep > 0, 1.0, 0.0)
    for m in range(4):
        weight_ref[m] = sums[m * 8 : m * 8 + 8] * wet
    lane = iota((ROWS, LANES), 1)
    sub = iota((ROWS, LANES), 0)
    nextq = (q + 1) & 31
    own, hot = [], []
    outside = jnp.full((ROWS, LANES), -1, jnp.int32)
    for r in range(4):
        line = jnp.broadcast_to(place_ref[pl.ds(r * 16 + (q >> 1), 1), :], (ROWS, LANES))
        place = jnp.take_along_axis(line, (lane >> 1) + 64 * (q & 1), axis=1)
        own.append(place)
        hot.append(jnp.where(jnp.broadcast_to(place[0:1] >> 8, (32, LANES)) == iota((32, LANES), 0), 1.0, 0.0))
        line = jnp.broadcast_to(place_ref[pl.ds(r * 16 + (nextq >> 1), 1), :], (ROWS, LANES))
        place = jnp.take_along_axis(line, (lane & 0) + 64 * (nextq & 1), axis=1)
        outside = jnp.where((lane >> 1) == r, place, outside)
    hot.append(jnp.where(jnp.broadcast_to(outside[0:1] >> 8, (32, LANES)) == iota((32, LANES), 0), 1.0, 0.0))
    owner = jnp.concatenate(hot, axis=1).astype(BF16)
    owner_ref[...] = owner
    stacked = jnp.concatenate(hot[:4], axis=0).astype(BF16)
    low, this = iota((LANES, LANES), 0), iota((LANES, LANES), 1)
    single = (low & 1) == 0
    before = jnp.where(single & ((low >> 1) < (this >> 1)), 1.0, 0.0).astype(BF16)
    every = jnp.where(single, 1.0, 0.0).astype(BF16)
    ahead = jnp.dot(stacked, before, preferred_element_type=F32)
    whole = jnp.dot(stacked, every, preferred_element_type=F32)
    carried = jnp.zeros((32, LANES), F32)
    slots = []
    for r in range(4):
        count = ahead[r * 32 : r * 32 + 32] + carried
        carried = carried + whole[r * 32 : r * 32 + 32]
        rank = jnp.sum(hot[r] * count, axis=0, keepdims=True).astype(jnp.int32)
        chosen = jnp.where(jnp.broadcast_to(rank, (ROWS, LANES)) == sub, 1.0, 0.0)
        rank_ref[r] = chosen
        slots.append(jnp.where((lane & 1) == 0, chosen * (own[r] & 255).astype(F32), 0.0))
    slots.append(jnp.zeros((ROWS, LANES), F32))
    main = jnp.concatenate(slots, axis=1)
    extra = jnp.where(lane == 2 * sub, (outside & 255).astype(F32), 0.0)
    extra = jnp.where(sub < 4, extra, 0.0)
    extra = jnp.concatenate([jnp.zeros((ROWS, 4 * LANES), F32), extra], axis=1)
    lines = jnp.concatenate(
        [jnp.zeros((24, 5 * LANES), F32), main, extra, jnp.zeros((88, 5 * LANES), F32)], axis=0
    ).astype(BF16)
    slot_ref[...] = lax.dot_general(owner, lines, (((1,), (1,)), ((), ())), preferred_element_type=F32)


def main_kernel(
    t_ref, s_ref, u_ref, v_ref, kap_ref, dep_ref, first_ref, second_ref, one_ref, two_ref,
    inv_ref, down_ref, up_ref, weight_ref, owner_ref, rank_ref, slot_ref,
    tout_ref, sout_ref, send_ref,
):
    shape = (ROWS, LANES)
    lane, sub = iota(shape, 1), iota(shape, 0)
    lane_first, lane_last = lane == 0, lane == LANES - 1
    row_first, row_last = sub == 0, sub == ROWS - 1
    mask = row_mask(lax.axis_index("gy") & 1)

    def ring(x, y, shift, axis, edge):
        rx, ry = pltpu.roll(x, shift, axis), pltpu.roll(y, shift, axis)
        return jnp.where(edge, ry, rx), jnp.where(edge, rx, ry)

    def east(f):
        a, b = ring(f[0], f[1], LANES - 1, 1, lane_last)
        h, g = ring(f[2], f[3], LANES - 1, 1, lane_last)
        return a, b, h, g

    def west(f):
        a, b = ring(f[0], f[1], 1, 1, lane_first)
        h, g = ring(f[2], f[3], 1, 1, lane_first)
        return a, b, h, g

    def north(f):
        a, h = ring(f[0], f[2], ROWS - 1, 0, row_last)
        b, g = ring(f[1], f[3], ROWS - 1, 0, row_last)
        return a, b, h, g

    def south(f):
        a, h = ring(f[0], f[2], 1, 0, row_first)
        b, g = ring(f[1], f[3], 1, 0, row_first)
        return a, b, h, g

    def pair(i):
        x, y = one_ref[i], two_ref[i]
        return jnp.where(mask, x, y), pltpu.roll(jnp.where(mask, y, x), 4, 0)

    side = side_columns(first_ref, second_ref)
    corner = []
    for i in range(3):
        corner.extend(pair(33 + i))

    def field(local, plane, k, outer):
        shift = (LANES - 8 * k - 4) % LANES
        return local, pltpu.roll(side[plane], shift, 1), outer, pltpu.roll(corner[plane], shift, 1)

    outer_kap, outer_dep = pair(32)
    kap = field(kap_ref[...], 4, 0, outer_kap)
    dep = field(dep_ref[...].astype(F32), 4, 1, outer_dep)
    kap_east = [0.5 * (x + y) for x, y in zip(kap, east(kap))]
    kap_north = [0.5 * (x + y) for x, y in zip(kap, north(kap))]
    dep_east = [jnp.minimum(x, y) for x, y in zip(dep, east(dep))]
    dep_north = [jnp.minimum(x, y) for x, y in zip(dep, north(dep))]

    def level(k, outer):
        u = field(u_ref[k], 2, k, outer[2])
        v = field(v_ref[k], 3, k, outer[3])
        level_f = float(k)

        def face(rate, kappa, depth):
            here = [
                jnp.where(d > level_f, jnp.maximum(r, 0.0) + c, 0.0) for r, c, d in zip(rate, kappa, depth)
            ]
            there = [
                jnp.where(d > level_f, c - jnp.minimum(r, 0.0), 0.0) for r, c, d in zip(rate, kappa, depth)
            ]
            return here, there

        here_e, from_e = face(u, kap_east, dep_east)
        here_n, from_n = face(v, kap_north, dep_north)
        from_w = west(here_e)
        from_s = south(here_n)
        back_e = west(from_e)
        back_n = south(from_n)
        keep = [
            1.0 - ((a + b) + (c + d)) for a, b, c, d in zip(here_e, back_e, here_n, back_n)
        ]
        for which, (in_ref, out_ref) in enumerate(((t_ref, tout_ref), (s_ref, sout_ref))):
            c = field(in_ref[k], which, k, outer[which])
            for step in range(NSUB):
                around = zip(keep, c, from_e, east(c), from_w, west(c), from_n, north(c), from_s, south(c))
                new = []
                for c0, x, ce, xe, cw, xw, cn, xn, cs, xs in around:
                    new.append((c0 * x + (ce * xe + cw * xw)) + (cn * xn + cs * xs))
                    if step == NSUB - 1:
                        break
                c = new
            out_ref[k] = c[0]

    for k in range(8):
        pairs = [pair(a * 8 + k) for a in range(4)]
        level(k, [p[0] for p in pairs])
        level(k + 8, [p[1] for p in pairs])

    tops = []
    for out_ref in (tout_ref, sout_ref):
        value = out_ref[0] * inv_ref[0]
        values = [value]
        for k in range(1, LEVELS):
            value = out_ref[k] * inv_ref[k] + down_ref[k] * value
            values.append(value)
        out_ref[LEVELS - 1] = value
        for k in range(LEVELS - 2, -1, -1):
            value = values[k] + up_ref[k] * value
            out_ref[k] = value
        tops.append(value)

    lines, extra = [], jnp.zeros(shape, F32)
    for t, top in enumerate(tops):
        moved = pltpu.roll(weight_ref[1] * top, 2, 1)
        beyond = lane < 2
        total = weight_ref[0] * top + jnp.where(beyond, 0.0, moved)
        total = total + pltpu.roll(weight_ref[2] * top, 2, 0)
        total = total + pltpu.roll(weight_ref[3] * top, ROWS - 2, 0)
        total = total + pltpu.roll(total, ROWS - 1, 0)
        moved = jnp.where(beyond, moved, 0.0)
        moved = moved + pltpu.roll(moved, ROWS - 1, 0)
        blocks = []
        for r in range(4):
            blocks.append(rank_ref[r] * jnp.broadcast_to(total[2 * r : 2 * r + 1], shape))
            line = jnp.broadcast_to(moved[2 * r : 2 * r + 1], shape)
            line = pltpu.roll(line, 2 * r, 1) if r else line
            extra = jnp.where(sub == 4 * t + r, line, extra)
        blocks.append(jnp.zeros(shape, F32))
        lines.append(jnp.concatenate(blocks, axis=1))
    lines.append(jnp.concatenate([jnp.zeros((ROWS, 4 * LANES), F32), extra], axis=1))
    rest = jnp.concatenate(lines, axis=0)
    owner = owner_ref[...]
    send = jnp.zeros((32, 24), F32)
    for _ in range(3):
        piece = rest.astype(BF16)
        rest = rest - piece.astype(F32)
        send = send + lax.dot_general(owner, piece, (((1,), (1,)), ((), ())), preferred_element_type=F32)
    send_ref[...] = slot_ref[...]
    send_ref[:, 0:24] = send


def owner_kernel(got_ref, air_ref):
    got = got_ref[...]
    shape = (32, LANES)
    lane = iota(shape, 1).astype(F32)
    sums = [[jnp.zeros(shape, F32) for _ in range(2)] for _ in range(2)]
    for j in range(12):
        first, second, place = (j, 8 + j, 24 + j) if j < 8 else (8 + j, 12 + j, 24 + j)
        slot = jnp.broadcast_to(got[:, place : place + 1], shape)
        terms = [jnp.broadcast_to(got[:, first : first + 1], shape), jnp.broadcast_to(got[:, second : second + 1], shape)]
        for half in range(2):
            hit = slot == lane + float(half * LANES)
            for t in range(2):
                sums[t][half] = sums[t][half] + jnp.where(hit, terms[t], 0.0)
    for t in range(2):
        for half in range(2):
            air_ref[t, :, half * LANES : half * LANES + LANES] = jnp.sum(sums[t][half], axis=0, keepdims=True)


VMEM = pl.BlockSpec(memory_space=pltpu.VMEM)


def call(kernel, name, outs, n_in, flops, **kw):
    return pl.pallas_call(
        kernel,
        name=name,
        out_shape=tuple(jax.ShapeDtypeStruct(s, d) for s, d in outs),
        in_specs=[VMEM] * n_in,
        out_specs=tuple([VMEM] * len(outs)),
        cost_estimate=pl.CostEstimate(flops=flops, bytes_accessed=1 << 20, transcendentals=0),
        compiler_params=pltpu.CompilerParams(vmem_limit_bytes=16 << 20),
        **kw,
    )


def shards(
    thermal_anomaly,
    saltiness_anomaly,
    zonal_volume_rate,
    meridional_volume_rate,
    sideways_diffusivity_factor,
    stratum_interface_mixing,
    flooded_strata,
    patch_sea_source,
    patch_sky_target,
    patch_measure_pointer,
    patch_measures,
    holder_ordering,
):
    nx, ny = lax.axis_size("gx"), lax.axis_size("gy")
    fields = (
        thermal_anomaly,
        saltiness_anomaly,
        zonal_volume_rate,
        meridional_volume_rate,
        sideways_diffusivity_factor,
        flooded_strata,
    )
    plane = (ROWS, LANES)
    strips = ((36,) + plane, F32)
    column, one, two = call(pack_kernel, "pack", [((5,) + plane, F32), strips, strips], 6, 1 << 20)(*fields)

    def swap(x, axis, count, start, wrap):
        pairs = []
        for i in range(start, count, 2):
            if i + 1 < count or wrap:
                pairs += [(i, (i + 1) % count), ((i + 1) % count, i)]
        return lax.ppermute(x, axis, pairs)

    first = swap(column, "gx", nx, 0, True)
    second = swap(column, "gx", nx, 1, True)
    one, two = call(corner_kernel, "corner", [strips, strips], 4, 1 << 16)(
        one, two, first, second
    )
    one = swap(one, "gy", ny, 0, False)
    two = swap(two, "gy", ny, 1, False)
    column3 = ((LEVELS,) + plane, F32)
    prepared = call(
        prep_kernel,
        "prep",
        [
            column3,
            column3,
            column3,
            ((4,) + plane, F32),
            ((32, 5 * LANES), BF16),
            ((4,) + plane, F32),
            ((32, LANES), F32),
        ],
        7,
        1 << 26,
    )(
        patch_sea_source.reshape(16, LANES),
        patch_sky_target.reshape(16, LANES),
        patch_measure_pointer.reshape(16, LANES),
        patch_measures.reshape(1, 64),
        holder_ordering.reshape(64, LANES),
        stratum_interface_mixing,
        flooded_strata,
    )
    temperature, salinity, send = call(
        main_kernel, "main", [column3, column3, ((32, LANES), F32)], 17, 1 << 24
    )(*fields, first, second, one, two, *prepared)
    got = lax.all_to_all(send.reshape(nx, 1, LANES), "gx", 0, 0, tiled=True)
    (air,) = call(owner_kernel, "owner", [((2, 1, 256), F32)], 1, 1 << 20)(got.reshape(nx, LANES))
    return temperature, salinity, air


def solution(mesh):
    placed = (
        P(None, "gy", "gx"),
        P(None, "gy", "gx"),
        P(None, "gy", "gx"),
        P(None, "gy", "gx"),
        P("gy", "gx"),
        P(None, "gy", "gx"),
        P("gy", "gx"),
        P("gy", "gx"),
        P("gy", "gx"),
        P("gy", "gx"),
        P(),
        P("gy", None),
    )
    return jax.shard_map(
        shards,
        mesh=mesh,
        in_specs=placed,
        out_specs=(P(None, "gy", "gx"), P(None, "gy", "gx"), P(None, "gy", "gx")),
        check_vma=False,
    )
```

```python
import jax
import jax.numpy as jnp
from jax import lax
from jax.experimental import pallas as pl
from jax.experimental.pallas import tpu as pltpu
from jax.sharding import PartitionSpec as P

NSUB = 4
LEVELS = 16
ROWS = 8
LANES = 128
F32 = jnp.float32
BF16 = jnp.bfloat16


LEAD = 20


def seat(place):
    return ((place >> 8) - LEAD) & 31


def iota(shape, dim):
    return lax.broadcasted_iota(jnp.int32, shape, dim)


def row_mask(parity):
    return (((iota((ROWS, LANES), 0) >> 2) + parity) & 1) == 0


def pack_kernel(*refs):
    sources, col_ref, held, sem = refs[:6], refs[6], refs[7:13], refs[13]
    copies = [pltpu.make_async_copy(x, y, sem.at[i]) for i, (x, y) in enumerate(zip(sources, held))]
    for copy in copies:
        copy.start()
    slot = iota((ROWS, LANES), 1) >> 3
    for a in range(4):
        copies[a].wait()
        strip = jnp.zeros((ROWS, LANES), F32)
        for k in range(LEVELS):
            strip = jnp.where(slot == k, pltpu.roll(held[a][k], (8 * k + 4) % LANES, 1), strip)
        col_ref[a] = strip
    copies[4].wait()
    copies[5].wait()
    strip = jnp.where(slot == 0, pltpu.roll(held[4][...], 4, 1), jnp.zeros((ROWS, LANES), F32))
    col_ref[4] = jnp.where(slot == 1, pltpu.roll(held[5][...].astype(F32), 12, 1), strip)


def side_columns(first_ref, second_ref):
    parity = lax.axis_index("gx") & 1
    mask = (((iota((ROWS, LANES), 1) >> 2) + parity) & 1) == 0
    return [jnp.where(mask, second_ref[a], first_ref[a]) for a in range(5)]


def rows_kernel(t_ref, s_ref, u_ref, v_ref, kap_ref, dep_ref, second_ref, first_ref, one_ref, two_ref):
    mask = row_mask(lax.axis_index("gy") & 1)

    def put(i, here, there):
        there = pltpu.roll(there, 4, 0)
        one_ref[i] = jnp.where(mask, there, here)
        two_ref[i] = jnp.where(mask, here, there)

    for a, ref in enumerate((t_ref, s_ref, u_ref, v_ref)):
        for k in range(8):
            put(a * 8 + k, ref[k], ref[k + 8])
    put(32, kap_ref[...], dep_ref[...].astype(F32))
    side = side_columns(first_ref, second_ref)
    side.append(jnp.zeros((ROWS, LANES), F32))
    for i in range(3):
        put(33 + i, side[2 * i], side[2 * i + 1])


def prep_kernel(
    src_ref, sky_ref, ptr_ref, area_ref, place_ref, mix_ref, dep_ref,
    inv_ref, down_ref, up_ref, weight_ref, owner_ref, rank_ref, slot_ref,
):
    q = lax.axis_index("gx")
    dep = dep_ref[...]
    above = jnp.zeros((ROWS, LANES), F32)
    carry = jnp.zeros((ROWS, LANES), F32)
    for k in range(LEVELS):
        below = jnp.where(dep > k + 1, mix_ref[k], 0.0) if k < LEVELS - 1 else jnp.zeros((ROWS, LANES), F32)
        inv = 1.0 / ((1.0 + above + below) - above * carry)
        carry = below * inv
        inv_ref[k] = inv
        down_ref[k] = above * inv
        up_ref[k] = carry
        above = below
    src = src_ref[...]
    sky = sky_ref[...]
    row, col = src >> 7, src & 127
    table = area_ref[...]
    table = jnp.broadcast_to(jnp.concatenate([table, table], axis=1), (16, LANES))
    area = jnp.take_along_axis(table, ptr_ref[...], axis=1)
    rise = (sky >> 11) - (row >> 1)
    east = ((sky & 2047) - (q * 64 + (col >> 1))) & 2047
    kind = jnp.where(east == 1, 1, jnp.where(rise == 1, 2, jnp.where(rise == -1, 3, 0)))
    high = kind * 8 + row
    part = []
    rest = area
    for _ in range(3):
        piece = rest.astype(BF16).astype(F32)
        part.append(piece)
        rest = rest - piece
    sums = jnp.zeros((96, LANES), F32)
    for i in range(0, 16, 2):
        left, right = [], []
        for j in (i, i + 1):
            hit = jnp.broadcast_to(high[j : j + 1], (32, LANES)) == iota((32, LANES), 0)
            left.append(
                jnp.concatenate(
                    [jnp.where(hit, jnp.broadcast_to(p[j : j + 1], (32, LANES)), 0.0) for p in part], axis=0
                )
            )
            same = jnp.broadcast_to(col[j : j + 1], (LANES, LANES)) == iota((LANES, LANES), 0)
            right.append(jnp.where(same, 1.0, 0.0))
        sums = sums + lax.dot_general(
            jnp.concatenate(left, axis=1).astype(BF16),
            jnp.concatenate(right, axis=1).astype(BF16),
            (((1,), (1,)), ((), ())),
            preferred_element_type=F32,
        )
    sums = sums[0:32] + sums[32:64] + sums[64:96]
    wet = jnp.where(dep > 0, 1.0, 0.0)
    for m in range(4):
        weight_ref[m] = sums[m * 8 : m * 8 + 8] * wet
    lane = iota((ROWS, LANES), 1)
    sub = iota((ROWS, LANES), 0)
    nextq = (q + 1) & 31
    own, hot = [], []
    outside = jnp.full((ROWS, LANES), -1, jnp.int32)
    for r in range(4):
        line = jnp.broadcast_to(place_ref[pl.ds(r * 16 + (q >> 1), 1), :], (ROWS, LANES))
        place = jnp.take_along_axis(line, (lane >> 1) + 64 * (q & 1), axis=1)
        own.append(place)
        hot.append(jnp.where(jnp.broadcast_to(seat(place[0:1]), (32, LANES)) == iota((32, LANES), 0), 1.0, 0.0))
        line = jnp.broadcast_to(place_ref[pl.ds(r * 16 + (nextq >> 1), 1), :], (ROWS, LANES))
        place = jnp.take_along_axis(line, (lane & 0) + 64 * (nextq & 1), axis=1)
        outside = jnp.where((lane >> 1) == r, place, outside)
    line = jnp.where(outside[0:1] < 0, -1, seat(outside[0:1]))
    hot.append(jnp.where(jnp.broadcast_to(line, (32, LANES)) == iota((32, LANES), 0), 1.0, 0.0))
    owner = jnp.concatenate(hot, axis=1).astype(BF16)
    owner_ref[...] = owner
    stacked = jnp.concatenate(hot[:4], axis=0).astype(BF16)
    low, this = iota((LANES, LANES), 0), iota((LANES, LANES), 1)
    single = (low & 1) == 0
    before = jnp.where(single & ((low >> 1) < (this >> 1)), 1.0, 0.0).astype(BF16)
    every = jnp.where(single, 1.0, 0.0).astype(BF16)
    ahead = jnp.dot(stacked, before, preferred_element_type=F32)
    whole = jnp.dot(stacked, every, preferred_element_type=F32)
    carried = jnp.zeros((32, LANES), F32)
    slots = []
    for r in range(4):
        count = ahead[r * 32 : r * 32 + 32] + carried
        carried = carried + whole[r * 32 : r * 32 + 32]
        rank = jnp.sum(hot[r] * count, axis=0, keepdims=True).astype(jnp.int32)
        chosen = jnp.where(jnp.broadcast_to(rank, (ROWS, LANES)) == sub, 1.0, 0.0)
        rank_ref[r] = chosen
        slots.append(jnp.where((lane & 1) == 0, chosen * (own[r] & 255).astype(F32), 0.0))
    slots.append(jnp.zeros((ROWS, LANES), F32))
    main = jnp.concatenate(slots, axis=1)
    extra = jnp.where(lane == 2 * sub, (outside & 255).astype(F32), 0.0)
    extra = jnp.where(sub < 4, extra, 0.0)
    extra = jnp.concatenate([jnp.zeros((ROWS, 4 * LANES), F32), extra], axis=1)
    lines = jnp.concatenate(
        [jnp.zeros((24, 5 * LANES), F32), main, extra, jnp.zeros((88, 5 * LANES), F32)], axis=0
    ).astype(BF16)
    slot_ref[...] = lax.dot_general(owner, lines, (((1,), (1,)), ((), ())), preferred_element_type=F32)


def main_kernel(
    t_ref, s_ref, u_ref, v_ref, kap_ref, dep_ref, second_ref, first_ref, two_ref, one_ref,
    inv_ref, down_ref, up_ref, weight_ref, owner_ref, rank_ref, slot_ref,
    tout_ref, sout_ref, send_ref,
):
    shape = (ROWS, LANES)
    lane, sub = iota(shape, 1), iota(shape, 0)
    lane_first, lane_last = lane == 0, lane == LANES - 1
    row_first, row_last = sub == 0, sub == ROWS - 1
    mask = row_mask(lax.axis_index("gy") & 1)

    def ring(x, y, shift, axis, edge):
        rx, ry = pltpu.roll(x, shift, axis), pltpu.roll(y, shift, axis)
        return jnp.where(edge, ry, rx), jnp.where(edge, rx, ry)

    def east(f):
        a, b = ring(f[0], f[1], LANES - 1, 1, lane_last)
        h, g = ring(f[2], f[3], LANES - 1, 1, lane_last)
        return a, b, h, g

    def west(f):
        a, b = ring(f[0], f[1], 1, 1, lane_first)
        h, g = ring(f[2], f[3], 1, 1, lane_first)
        return a, b, h, g

    def north(f):
        a, h = ring(f[0], f[2], ROWS - 1, 0, row_last)
        b, g = ring(f[1], f[3], ROWS - 1, 0, row_last)
        return a, b, h, g

    def south(f):
        a, h = ring(f[0], f[2], 1, 0, row_first)
        b, g = ring(f[1], f[3], 1, 0, row_first)
        return a, b, h, g

    def pair(i):
        x, y = one_ref[i], two_ref[i]
        return jnp.where(mask, x, y), pltpu.roll(jnp.where(mask, y, x), 4, 0)

    side = side_columns(first_ref, second_ref)
    corner = []
    for i in range(3):
        corner.extend(pair(33 + i))

    def field(local, plane, k, outer):
        shift = (LANES - 8 * k - 4) % LANES
        return local, pltpu.roll(side[plane], shift, 1), outer, pltpu.roll(corner[plane], shift, 1)

    outer_kap, outer_dep = pair(32)
    kap = field(kap_ref[...], 4, 0, outer_kap)
    dep = field(dep_ref[...].astype(F32), 4, 1, outer_dep)
    kap_east = [0.5 * (x + y) for x, y in zip(kap, east(kap))]
    kap_north = [0.5 * (x + y) for x, y in zip(kap, north(kap))]
    dep_east = [jnp.minimum(x, y) for x, y in zip(dep, east(dep))]
    dep_north = [jnp.minimum(x, y) for x, y in zip(dep, north(dep))]

    def level(k, outer):
        u = field(u_ref[k], 2, k, outer[2])
        v = field(v_ref[k], 3, k, outer[3])
        level_f = float(k)

        def face(rate, kappa, depth):
            here = [
                jnp.where(d > level_f, jnp.maximum(r, 0.0) + c, 0.0) for r, c, d in zip(rate, kappa, depth)
            ]
            there = [
                jnp.where(d > level_f, c - jnp.minimum(r, 0.0), 0.0) for r, c, d in zip(rate, kappa, depth)
            ]
            return here, there

        here_e, from_e = face(u, kap_east, dep_east)
        here_n, from_n = face(v, kap_north, dep_north)
        from_w = west(here_e)
        from_s = south(here_n)
        back_e = west(from_e)
        back_n = south(from_n)
        keep = [
            1.0 - ((a + b) + (c + d)) for a, b, c, d in zip(here_e, back_e, here_n, back_n)
        ]
        for which, (in_ref, out_ref) in enumerate(((t_ref, tout_ref), (s_ref, sout_ref))):
            c = field(in_ref[k], which, k, outer[which])
            for step in range(NSUB):
                around = zip(keep, c, from_e, east(c), from_w, west(c), from_n, north(c), from_s, south(c))
                new = []
                for c0, x, ce, xe, cw, xw, cn, xn, cs, xs in around:
                    new.append((c0 * x + (ce * xe + cw * xw)) + (cn * xn + cs * xs))
                    if step == NSUB - 1:
                        break
                c = new
            out_ref[k] = c[0]

    for k in range(8):
        pairs = [pair(a * 8 + k) for a in range(4)]
        level(k, [p[0] for p in pairs])
        level(k + 8, [p[1] for p in pairs])

    tops = []
    for out_ref in (tout_ref, sout_ref):
        value = out_ref[0] * inv_ref[0]
        values = [value]
        for k in range(1, LEVELS):
            value = out_ref[k] * inv_ref[k] + down_ref[k] * value
            values.append(value)
        out_ref[LEVELS - 1] = value
        for k in range(LEVELS - 2, -1, -1):
            value = values[k] + up_ref[k] * value
            out_ref[k] = value
        tops.append(value)

    lines, extra = [], jnp.zeros(shape, F32)
    for t, top in enumerate(tops):
        moved = pltpu.roll(weight_ref[1] * top, 2, 1)
        beyond = lane < 2
        total = weight_ref[0] * top + jnp.where(beyond, 0.0, moved)
        total = total + pltpu.roll(weight_ref[2] * top, 2, 0)
        total = total + pltpu.roll(weight_ref[3] * top, ROWS - 2, 0)
        total = total + pltpu.roll(total, ROWS - 1, 0)
        moved = jnp.where(beyond, moved, 0.0)
        moved = moved + pltpu.roll(moved, ROWS - 1, 0)
        blocks = []
        for r in range(4):
            blocks.append(rank_ref[r] * jnp.broadcast_to(total[2 * r : 2 * r + 1], shape))
            line = jnp.broadcast_to(moved[2 * r : 2 * r + 1], shape)
            line = pltpu.roll(line, 2 * r, 1) if r else line
            extra = jnp.where(sub == 4 * t + r, line, extra)
        blocks.append(jnp.zeros(shape, F32))
        lines.append(jnp.concatenate(blocks, axis=1))
    lines.append(jnp.concatenate([jnp.zeros((ROWS, 4 * LANES), F32), extra], axis=1))
    rest = jnp.concatenate(lines, axis=0)
    owner = owner_ref[...]
    send = jnp.zeros((32, 24), F32)
    for _ in range(3):
        piece = rest.astype(BF16)
        rest = rest - piece.astype(F32)
        send = send + lax.dot_general(owner, piece, (((1,), (1,)), ((), ())), preferred_element_type=F32)
    send_ref[...] = slot_ref[...]
    send_ref[:, 0:24] = send


def owner_kernel(got_ref, air_ref):
    got = got_ref[...]
    shape = (32, LANES)
    lane = iota(shape, 1).astype(F32)
    sums = [[jnp.zeros(shape, F32) for _ in range(2)] for _ in range(2)]
    for j in range(12):
        first, second, place = (j, 8 + j, 24 + j) if j < 8 else (8 + j, 12 + j, 24 + j)
        slot = jnp.broadcast_to(got[:, place : place + 1], shape)
        terms = [jnp.broadcast_to(got[:, first : first + 1], shape), jnp.broadcast_to(got[:, second : second + 1], shape)]
        for half in range(2):
            hit = slot == lane + float(half * LANES)
            for t in range(2):
                sums[t][half] = sums[t][half] + jnp.where(hit, terms[t], 0.0)
    for t in range(2):
        for half in range(2):
            air_ref[t, :, half * LANES : half * LANES + LANES] = jnp.sum(sums[t][half], axis=0, keepdims=True)


VMEM = pl.BlockSpec(memory_space=pltpu.VMEM)


def call(kernel, name, outs, n_in, flops, **kw):
    kw.setdefault("in_specs", [VMEM] * n_in)
    kw.setdefault("compiler_params", pltpu.CompilerParams(vmem_limit_bytes=16 << 20))
    return pl.pallas_call(
        kernel,
        name=name,
        out_shape=tuple(jax.ShapeDtypeStruct(s, d) for s, d in outs),
        out_specs=tuple([VMEM] * len(outs)),
        cost_estimate=pl.CostEstimate(flops=flops, bytes_accessed=1 << 20, transcendentals=0),
        **kw,
    )


def shards(
    thermal_anomaly,
    saltiness_anomaly,
    zonal_volume_rate,
    meridional_volume_rate,
    sideways_diffusivity_factor,
    stratum_interface_mixing,
    flooded_strata,
    patch_sea_source,
    patch_sky_target,
    patch_measure_pointer,
    patch_measures,
    holder_ordering,
):
    nx, ny = lax.axis_size("gx"), lax.axis_size("gy")
    fields = (
        thermal_anomaly,
        saltiness_anomaly,
        zonal_volume_rate,
        meridional_volume_rate,
        sideways_diffusivity_factor,
        flooded_strata,
    )
    plane = (ROWS, LANES)
    strips = ((36,) + plane, F32)
    (column,) = call(
        pack_kernel,
        "pack",
        [((5,) + plane, F32)],
        6,
        1 << 18,
        in_specs=[pl.BlockSpec(memory_space=pltpu.HBM)] * 6,
        scratch_shapes=[pltpu.VMEM(x.shape, x.dtype) for x in fields] + [pltpu.SemaphoreType.DMA((6,))],
        compiler_params=None,
    )(*fields)

    def swap(x, axis, count, start, wrap):
        pairs = []
        for i in range(start, count, 2):
            if i + 1 < count or wrap:
                pairs += [(i, (i + 1) % count), ((i + 1) % count, i)]
        return lax.ppermute(x, axis, pairs)

    second = swap(column, "gx", nx, 1, True)
    first = swap(column, "gx", nx, 0, True)
    one, two = call(rows_kernel, "rows", [strips, strips], 8, 1 << 16)(*fields, second, first)
    two = swap(two, "gy", ny, 1, False)
    one = swap(one, "gy", ny, 0, False)
    column3 = ((LEVELS,) + plane, F32)
    prepared = call(
        prep_kernel,
        "prep",
        [
            column3,
            column3,
            column3,
            ((4,) + plane, F32),
            ((32, 5 * LANES), BF16),
            ((4,) + plane, F32),
            ((32, LANES), F32),
        ],
        7,
        1 << 26,
    )(
        patch_sea_source.reshape(16, LANES),
        patch_sky_target.reshape(16, LANES),
        patch_measure_pointer.reshape(16, LANES),
        patch_measures.reshape(1, 64),
        holder_ordering.reshape(64, LANES),
        stratum_interface_mixing,
        flooded_strata,
    )
    temperature, salinity, send = call(
        main_kernel, "main", [column3, column3, ((32, LANES), F32)], 17, 1 << 24
    )(*fields, second, first, two, one, *prepared)
    order = [[(i + LEAD) % nx for i in range(nx)]]
    got = lax.all_to_all(send.reshape(nx, 1, LANES), "gx", 0, 0, tiled=True, axis_index_groups=order)
    (air,) = call(owner_kernel, "owner", [((2, 1, 256), F32)], 1, 1 << 20)(got.reshape(nx, LANES))
    return temperature, salinity, air


def solution(mesh):
    placed = (
        P(None, "gy", "gx"),
        P(None, "gy", "gx"),
        P(None, "gy", "gx"),
        P(None, "gy", "gx"),
        P("gy", "gx"),
        P(None, "gy", "gx"),
        P("gy", "gx"),
        P("gy", "gx"),
        P("gy", "gx"),
        P("gy", "gx"),
        P(),
        P("gy", None),
    )
    return jax.shard_map(
        shards,
        mesh=mesh,
        in_specs=placed,
        out_specs=(P(None, "gy", "gx"), P(None, "gy", "gx"), P(None, "gy", "gx")),
        check_vma=False,
    )
```

```python
import jax
import jax.numpy as jnp
from jax import lax
from jax.experimental import pallas as pl
from jax.experimental.pallas import tpu as pltpu
from jax.sharding import PartitionSpec as P

NSUB = 4
LEVELS = 16
ROWS = 8
LANES = 128
F32 = jnp.float32
BF16 = jnp.bfloat16


LEAD = 20


def seat(place):
    return ((place >> 8) - LEAD) & 31


def iota(shape, dim):
    return lax.broadcasted_iota(jnp.int32, shape, dim)


def row_mask(parity):
    return (((iota((ROWS, LANES), 0) >> 2) + parity) & 1) == 0


def pack_kernel(*refs):
    sources, col_ref, held, sem = refs[:6], refs[6], refs[7:13], refs[13]
    copies = [pltpu.make_async_copy(x, y, sem.at[i]) for i, (x, y) in enumerate(zip(sources, held))]
    for copy in copies:
        copy.start()
    slot = iota((ROWS, LANES), 1) >> 3
    for a in range(4):
        copies[a].wait()
        strip = jnp.zeros((ROWS, LANES), F32)
        for k in range(LEVELS):
            strip = jnp.where(slot == k, pltpu.roll(held[a][k], (8 * k + 4) % LANES, 1), strip)
        col_ref[a] = strip
    copies[4].wait()
    copies[5].wait()
    strip = jnp.where(slot == 0, pltpu.roll(held[4][...], 4, 1), jnp.zeros((ROWS, LANES), F32))
    col_ref[4] = jnp.where(slot == 1, pltpu.roll(held[5][...].astype(F32), 12, 1), strip)


def side_columns(first_ref, second_ref):
    parity = lax.axis_index("gx") & 1
    mask = (((iota((ROWS, LANES), 1) >> 2) + parity) & 1) == 0
    return [jnp.where(mask, second_ref[a], first_ref[a]) for a in range(5)]


def rows_kernel(t_ref, s_ref, u_ref, v_ref, kap_ref, dep_ref, second_ref, first_ref, one_ref, two_ref):
    mask = row_mask(lax.axis_index("gy") & 1)

    def put(i, here, there):
        there = pltpu.roll(there, 4, 0)
        one_ref[i] = jnp.where(mask, there, here)
        two_ref[i] = jnp.where(mask, here, there)

    for a, ref in enumerate((t_ref, s_ref, u_ref, v_ref)):
        for k in range(8):
            put(a * 8 + k, ref[k], ref[k + 8])
    put(32, kap_ref[...], dep_ref[...].astype(F32))
    side = side_columns(first_ref, second_ref)
    side.append(jnp.zeros((ROWS, LANES), F32))
    for i in range(3):
        put(33 + i, side[2 * i], side[2 * i + 1])


def prep_kernel(
    src_ref, sky_ref, ptr_ref, area_ref, place_ref, mix_ref, dep_ref,
    inv_ref, down_ref, up_ref, weight_ref, owner_ref, rank_ref, slot_ref,
):
    q = lax.axis_index("gx")
    dep = dep_ref[...]
    above = jnp.zeros((ROWS, LANES), F32)
    carry = jnp.zeros((ROWS, LANES), F32)
    for k in range(LEVELS):
        below = jnp.where(dep > k + 1, mix_ref[k], 0.0) if k < LEVELS - 1 else jnp.zeros((ROWS, LANES), F32)
        inv = 1.0 / ((1.0 + above + below) - above * carry)
        carry = below * inv
        inv_ref[k] = inv
        down_ref[k] = above * inv
        up_ref[k] = carry
        above = below
    src = src_ref[...]
    sky = sky_ref[...]
    row, col = src >> 7, src & 127
    table = area_ref[...]
    table = jnp.broadcast_to(jnp.concatenate([table, table], axis=1), (16, LANES))
    area = jnp.take_along_axis(table, ptr_ref[...], axis=1)
    rise = (sky >> 11) - (row >> 1)
    east = ((sky & 2047) - (q * 64 + (col >> 1))) & 2047
    kind = jnp.where(east == 1, 1, jnp.where(rise == 1, 2, jnp.where(rise == -1, 3, 0)))
    high = kind * 8 + row
    part = []
    rest = area
    for _ in range(3):
        piece = rest.astype(BF16).astype(F32)
        part.append(piece)
        rest = rest - piece
    sums = jnp.zeros((96, LANES), F32)
    for i in range(0, 16, 2):
        left, right = [], []
        for j in (i, i + 1):
            hit = jnp.broadcast_to(high[j : j + 1], (32, LANES)) == iota((32, LANES), 0)
            left.append(
                jnp.concatenate(
                    [jnp.where(hit, jnp.broadcast_to(p[j : j + 1], (32, LANES)), 0.0) for p in part], axis=0
                )
            )
            same = jnp.broadcast_to(col[j : j + 1], (LANES, LANES)) == iota((LANES, LANES), 0)
            right.append(jnp.where(same, 1.0, 0.0))
        sums = sums + lax.dot_general(
            jnp.concatenate(left, axis=1).astype(BF16),
            jnp.concatenate(right, axis=1).astype(BF16),
            (((1,), (1,)), ((), ())),
            preferred_element_type=F32,
        )
    sums = sums[0:32] + sums[32:64] + sums[64:96]
    wet = jnp.where(dep > 0, 1.0, 0.0)
    for m in range(4):
        weight_ref[m] = sums[m * 8 : m * 8 + 8] * wet
    lane = iota((ROWS, LANES), 1)
    sub = iota((ROWS, LANES), 0)
    nextq = (q + 1) & 31
    own, hot = [], []
    outside = jnp.full((ROWS, LANES), -1, jnp.int32)
    for r in range(4):
        line = jnp.broadcast_to(place_ref[pl.ds(r * 16 + (q >> 1), 1), :], (ROWS, LANES))
        place = jnp.take_along_axis(line, (lane >> 1) + 64 * (q & 1), axis=1)
        own.append(place)
        hot.append(jnp.where(jnp.broadcast_to(seat(place[0:1]), (32, LANES)) == iota((32, LANES), 0), 1.0, 0.0))
        line = jnp.broadcast_to(place_ref[pl.ds(r * 16 + (nextq >> 1), 1), :], (ROWS, LANES))
        place = jnp.take_along_axis(line, (lane & 0) + 64 * (nextq & 1), axis=1)
        outside = jnp.where((lane >> 1) == r, place, outside)
    line = jnp.where(outside[0:1] < 0, -1, seat(outside[0:1]))
    hot.append(jnp.where(jnp.broadcast_to(line, (32, LANES)) == iota((32, LANES), 0), 1.0, 0.0))
    owner = jnp.concatenate(hot, axis=1).astype(BF16)
    owner_ref[...] = owner
    stacked = jnp.concatenate(hot[:4], axis=0).astype(BF16)
    low, this = iota((LANES, LANES), 0), iota((LANES, LANES), 1)
    single = (low & 1) == 0
    before = jnp.where(single & ((low >> 1) < (this >> 1)), 1.0, 0.0).astype(BF16)
    every = jnp.where(single, 1.0, 0.0).astype(BF16)
    ahead = jnp.dot(stacked, before, preferred_element_type=F32)
    whole = jnp.dot(stacked, every, preferred_element_type=F32)
    carried = jnp.zeros((32, LANES), F32)
    slots = []
    for r in range(4):
        count = ahead[r * 32 : r * 32 + 32] + carried
        carried = carried + whole[r * 32 : r * 32 + 32]
        rank = jnp.sum(hot[r] * count, axis=0, keepdims=True).astype(jnp.int32)
        chosen = jnp.where(jnp.broadcast_to(rank, (ROWS, LANES)) == sub, 1.0, 0.0)
        rank_ref[r] = chosen
        slots.append(jnp.where((lane & 1) == 0, chosen * (own[r] & 255).astype(F32), 0.0))
    slots.append(jnp.zeros((ROWS, LANES), F32))
    main = jnp.concatenate(slots, axis=1)
    extra = jnp.where(lane == 2 * sub, (outside & 255).astype(F32), 0.0)
    extra = jnp.where(sub < 4, extra, 0.0)
    extra = jnp.concatenate([jnp.zeros((ROWS, 4 * LANES), F32), extra], axis=1)
    lines = jnp.concatenate(
        [jnp.zeros((24, 5 * LANES), F32), main, extra, jnp.zeros((88, 5 * LANES), F32)], axis=0
    ).astype(BF16)
    slot_ref[...] = lax.dot_general(owner, lines, (((1,), (1,)), ((), ())), preferred_element_type=F32)


def main_kernel(
    t_ref, s_ref, u_ref, v_ref, kap_ref, dep_ref, second_ref, first_ref, two_ref, one_ref,
    inv_ref, down_ref, up_ref, weight_ref, owner_ref, rank_ref, slot_ref,
    tout_ref, sout_ref, send_ref, strip_ref, face_ref,
):
    shape = (ROWS, LANES)
    lane, sub = iota(shape, 1), iota(shape, 0)
    lane_first, lane_last = lane == 0, lane == LANES - 1
    row_first, row_last = sub == 0, sub == ROWS - 1
    mask = row_mask(lax.axis_index("gy") & 1)

    def ring(x, y, shift, axis, edge):
        rx, ry = pltpu.roll(x, shift, axis), pltpu.roll(y, shift, axis)
        return jnp.where(edge, ry, rx), jnp.where(edge, rx, ry)

    def east(f):
        a, b = ring(f[0], f[1], LANES - 1, 1, lane_last)
        h, g = ring(f[2], f[3], LANES - 1, 1, lane_last)
        return a, b, h, g

    def west(f):
        a, b = ring(f[0], f[1], 1, 1, lane_first)
        h, g = ring(f[2], f[3], 1, 1, lane_first)
        return a, b, h, g

    def north(f):
        a, h = ring(f[0], f[2], ROWS - 1, 0, row_last)
        b, g = ring(f[1], f[3], ROWS - 1, 0, row_last)
        return a, b, h, g

    def south(f):
        a, h = ring(f[0], f[2], 1, 0, row_first)
        b, g = ring(f[1], f[3], 1, 0, row_first)
        return a, b, h, g

    def pair(i):
        x, y = one_ref[i], two_ref[i]
        return jnp.where(mask, x, y), pltpu.roll(jnp.where(mask, y, x), 4, 0)

    side = side_columns(first_ref, second_ref)
    corner = []
    for i in range(3):
        corner.extend(pair(33 + i))

    for i in range(5):
        strip_ref[0, i] = side[i]
        strip_ref[1, i] = corner[i]

    def field(local, plane, k, outer):
        shift = (2 * LANES - 8 * k - 4) % LANES if isinstance(k, int) else (2 * LANES - 4) - 8 * k
        strips = [pltpu.roll(strip_ref[i, plane], shift, 1) for i in range(2)]
        return local, strips[0], outer, strips[1]

    outer_kap, outer_dep = pair(32)
    kap = field(kap_ref[...], 4, 0, outer_kap)
    dep = field(dep_ref[...].astype(F32), 4, 1, outer_dep)
    faces = (
        [0.5 * (x + y) for x, y in zip(kap, east(kap))],
        [0.5 * (x + y) for x, y in zip(kap, north(kap))],
        [jnp.minimum(x, y) for x, y in zip(dep, east(dep))],
        [jnp.minimum(x, y) for x, y in zip(dep, north(dep))],
    )
    for i, face in enumerate(faces):
        for j in range(4):
            face_ref[i, j] = face[j]

    def level(k, outer):
        u = field(u_ref[k], 2, k, outer[2])
        v = field(v_ref[k], 3, k, outer[3])
        level_f = lax.convert_element_type(k, F32)

        def face(rate, which):
            here, there = [], []
            for i, r in enumerate(rate):
                c = face_ref[which, i]
                wet = face_ref[which + 2, i] > level_f
                here.append(jnp.where(wet, jnp.maximum(r, 0.0) + c, 0.0))
                there.append(jnp.where(wet, c - jnp.minimum(r, 0.0), 0.0))
            return here, there

        here_e, from_e = face(u, 0)
        here_n, from_n = face(v, 1)
        from_w = west(here_e)
        from_s = south(here_n)
        back_e = west(from_e)
        back_n = south(from_n)
        keep = [1.0 - ((a + b) + (c + d)) for a, b, c, d in zip(here_e, back_e, here_n, back_n)]
        cells = [field(ref[k], i, k, outer[i]) for i, ref in enumerate((t_ref, s_ref))]
        for step in range(NSUB):
            for i, c in enumerate(cells):
                around = zip(keep, c, from_e, east(c), from_w, west(c), from_n, north(c), from_s, south(c))
                new = []
                for c0, x, ce, xe, cw, xw, cn, xn, cs, xs in around:
                    new.append((c0 * x + (ce * xe + cw * xw)) + (cn * xn + cs * xs))
                    if step == NSUB - 1:
                        break
                cells[i] = new
        tout_ref[k] = cells[0][0]
        sout_ref[k] = cells[1][0]

    def two_levels(k, nothing):
        pairs = [pair(a * 8 + k) for a in range(4)]
        level(k, [p[0] for p in pairs])
        level(k + 8, [p[1] for p in pairs])
        return nothing

    lax.fori_loop(0, 8, two_levels, 0, unroll=2)

    tops = []
    for out_ref in (tout_ref, sout_ref):
        value = out_ref[0] * inv_ref[0]
        values = [value]
        for k in range(1, LEVELS):
            value = out_ref[k] * inv_ref[k] + down_ref[k] * value
            values.append(value)
        out_ref[LEVELS - 1] = value
        for k in range(LEVELS - 2, -1, -1):
            value = values[k] + up_ref[k] * value
            out_ref[k] = value
        tops.append(value)

    lines, extra = [], jnp.zeros(shape, F32)
    for t, top in enumerate(tops):
        moved = pltpu.roll(weight_ref[1] * top, 2, 1)
        beyond = lane < 2
        total = weight_ref[0] * top + jnp.where(beyond, 0.0, moved)
        total = total + pltpu.roll(weight_ref[2] * top, 2, 0)
        total = total + pltpu.roll(weight_ref[3] * top, ROWS - 2, 0)
        total = total + pltpu.roll(total, ROWS - 1, 0)
        moved = jnp.where(beyond, moved, 0.0)
        moved = moved + pltpu.roll(moved, ROWS - 1, 0)
        blocks = []
        for r in range(4):
            blocks.append(rank_ref[r] * jnp.broadcast_to(total[2 * r : 2 * r + 1], shape))
            line = jnp.broadcast_to(moved[2 * r : 2 * r + 1], shape)
            line = pltpu.roll(line, 2 * r, 1) if r else line
            extra = jnp.where(sub == 4 * t + r, line, extra)
        blocks.append(jnp.zeros(shape, F32))
        lines.append(jnp.concatenate(blocks, axis=1))
    lines.append(jnp.concatenate([jnp.zeros((ROWS, 4 * LANES), F32), extra], axis=1))
    rest = jnp.concatenate(lines, axis=0)
    owner = owner_ref[...]
    send = jnp.zeros((32, 24), F32)
    for _ in range(3):
        piece = rest.astype(BF16)
        rest = rest - piece.astype(F32)
        send = send + lax.dot_general(owner, piece, (((1,), (1,)), ((), ())), preferred_element_type=F32)
    send_ref[...] = slot_ref[...]
    send_ref[:, 0:24] = send


def owner_kernel(got_ref, air_ref):
    got = got_ref[...]
    shape = (32, LANES)
    lane = iota(shape, 1).astype(F32)
    sums = [[jnp.zeros(shape, F32) for _ in range(2)] for _ in range(2)]
    for j in range(12):
        first, second, place = (j, 8 + j, 24 + j) if j < 8 else (8 + j, 12 + j, 24 + j)
        slot = jnp.broadcast_to(got[:, place : place + 1], shape)
        terms = [jnp.broadcast_to(got[:, first : first + 1], shape), jnp.broadcast_to(got[:, second : second + 1], shape)]
        for half in range(2):
            hit = slot == lane + float(half * LANES)
            for t in range(2):
                sums[t][half] = sums[t][half] + jnp.where(hit, terms[t], 0.0)
    for t in range(2):
        for half in range(2):
            air_ref[t, :, half * LANES : half * LANES + LANES] = jnp.sum(sums[t][half], axis=0, keepdims=True)


VMEM = pl.BlockSpec(memory_space=pltpu.VMEM)


def call(kernel, name, outs, n_in, flops, **kw):
    kw.setdefault("in_specs", [VMEM] * n_in)
    kw.setdefault("compiler_params", pltpu.CompilerParams(vmem_limit_bytes=16 << 20))
    return pl.pallas_call(
        kernel,
        name=name,
        out_shape=tuple(jax.ShapeDtypeStruct(s, d) for s, d in outs),
        out_specs=tuple([VMEM] * len(outs)),
        cost_estimate=pl.CostEstimate(flops=flops, bytes_accessed=1 << 20, transcendentals=0),
        **kw,
    )


def shards(
    thermal_anomaly,
    saltiness_anomaly,
    zonal_volume_rate,
    meridional_volume_rate,
    sideways_diffusivity_factor,
    stratum_interface_mixing,
    flooded_strata,
    patch_sea_source,
    patch_sky_target,
    patch_measure_pointer,
    patch_measures,
    holder_ordering,
):
    nx, ny = lax.axis_size("gx"), lax.axis_size("gy")
    fields = (
        thermal_anomaly,
        saltiness_anomaly,
        zonal_volume_rate,
        meridional_volume_rate,
        sideways_diffusivity_factor,
        flooded_strata,
    )
    plane = (ROWS, LANES)
    strips = ((36,) + plane, F32)
    column, *held = call(
        pack_kernel,
        "pack",
        [((5,) + plane, F32)] + [(x.shape, x.dtype) for x in fields],
        6,
        1 << 18,
        in_specs=[pl.BlockSpec(memory_space=pltpu.HBM)] * 6,
        scratch_shapes=[pltpu.SemaphoreType.DMA((6,))],
    )(*[pltpu.with_memory_space_constraint(x, pltpu.HBM) for x in fields])

    def swap(x, axis, count, start, wrap):
        pairs = []
        for i in range(start, count, 2):
            if i + 1 < count or wrap:
                pairs += [(i, (i + 1) % count), ((i + 1) % count, i)]
        return lax.ppermute(x, axis, pairs)

    second = swap(column, "gx", nx, 1, True)
    first = swap(column, "gx", nx, 0, True)
    one, two = call(rows_kernel, "rows", [strips, strips], 8, 1 << 16)(*held, second, first)
    two = swap(two, "gy", ny, 1, False)
    one = swap(one, "gy", ny, 0, False)
    column3 = ((LEVELS,) + plane, F32)
    prepared = call(
        prep_kernel,
        "prep",
        [
            column3,
            column3,
            column3,
            ((4,) + plane, F32),
            ((32, 5 * LANES), BF16),
            ((4,) + plane, F32),
            ((32, LANES), F32),
        ],
        7,
        1 << 26,
    )(
        patch_sea_source.reshape(16, LANES),
        patch_sky_target.reshape(16, LANES),
        patch_measure_pointer.reshape(16, LANES),
        patch_measures.reshape(1, 64),
        holder_ordering.reshape(64, LANES),
        stratum_interface_mixing,
        held[5],
    )
    temperature, salinity, send = call(
        main_kernel,
        "main",
        [column3, column3, ((32, LANES), F32)],
        17,
        1 << 24,
        scratch_shapes=[pltpu.VMEM((2, 5) + plane, F32), pltpu.VMEM((4, 4) + plane, F32)],
    )(*held, second, first, two, one, *prepared)
    order = [[(i + LEAD) % nx for i in range(nx)]]
    got = lax.all_to_all(send.reshape(nx, 1, LANES), "gx", 0, 0, tiled=True, axis_index_groups=order)
    (air,) = call(owner_kernel, "owner", [((2, 1, 256), F32)], 1, 1 << 20)(got.reshape(nx, LANES))
    return temperature, salinity, air


def solution(mesh):
    placed = (
        P(None, "gy", "gx"),
        P(None, "gy", "gx"),
        P(None, "gy", "gx"),
        P(None, "gy", "gx"),
        P("gy", "gx"),
        P(None, "gy", "gx"),
        P("gy", "gx"),
        P("gy", "gx"),
        P("gy", "gx"),
        P("gy", "gx"),
        P(),
        P("gy", None),
    )
    return jax.shard_map(
        shards,
        mesh=mesh,
        in_specs=placed,
        out_specs=(P(None, "gy", "gx"), P(None, "gy", "gx"), P(None, "gy", "gx")),
        check_vma=False,
    )
```

```python
import jax
import jax.numpy as jnp
from jax import lax
from jax.experimental import pallas as pl
from jax.experimental.pallas import tpu as pltpu
from jax.sharding import PartitionSpec as P

NSUB = 4
LEVELS = 16
ROWS = 8
LANES = 128
F32 = jnp.float32
BF16 = jnp.bfloat16


LEAD = 20


def seat(place):
    return ((place >> 8) - LEAD) & 31


def iota(shape, dim):
    return lax.broadcasted_iota(jnp.int32, shape, dim)


def row_mask(parity):
    return (((iota((ROWS, LANES), 0) >> 2) + parity) & 1) == 0


def strips(planes):
    slot = iota((ROWS, LANES), 1) >> 3
    strip = jnp.zeros((ROWS, LANES), F32)
    for k, plane in enumerate(planes):
        strip = jnp.where(slot == k, pltpu.roll(plane, (8 * k + 4) % LANES, 1), strip)
    return strip


def rows_kernel(*refs):
    sources, (one_ref, two_ref), held, sem = refs[:6], refs[6:8], refs[8:14], refs[14]
    copies = [pltpu.make_async_copy(x, y, sem.at[i]) for i, (x, y) in enumerate(zip(sources, held))]
    for copy in copies:
        copy.start()
    mask = row_mask(lax.axis_index("gy") & 1)

    def put(i, here, there):
        there = pltpu.roll(there, 4, 0)
        one_ref[i] = jnp.where(mask, there, here)
        two_ref[i] = jnp.where(mask, here, there)

    for a in range(4):
        copies[a].wait()
        for k in range(8):
            put(a * 8 + k, held[a][k], held[a][k + 8])
    copies[4].wait()
    copies[5].wait()
    put(32, held[4][...], held[5][...].astype(F32))


def unpair(i, mask, one_ref, two_ref):
    x, y = one_ref[i], two_ref[i]
    return jnp.where(mask, x, y), pltpu.roll(jnp.where(mask, y, x), 4, 0)


def columns_kernel(local_ref, two_ref, one_ref, col_ref):
    mask = row_mask(lax.axis_index("gy") & 1)
    for a in range(4):
        pairs = [unpair(a * 8 + k, mask, one_ref, two_ref) for k in range(8)]
        col_ref[a] = local_ref[a]
        col_ref[5 + a] = strips([x[0] for x in pairs] + [x[1] for x in pairs])
    col_ref[4] = local_ref[4]
    col_ref[9] = strips(unpair(32, mask, one_ref, two_ref))


def side_columns(first_ref, second_ref):
    parity = lax.axis_index("gx") & 1
    mask = (((iota((ROWS, LANES), 1) >> 2) + parity) & 1) == 0
    return [jnp.where(mask, second_ref[a], first_ref[a]) for a in range(10)]


def prep_kernel(
    src_ref, sky_ref, ptr_ref, area_ref, place_ref, mix_ref, t_ref, s_ref, u_ref, v_ref, kap_ref, dep_ref,
    inv_ref, down_ref, up_ref, weight_ref, owner_ref, rank_ref, slot_ref, col_ref,
):
    for a, ref in enumerate((t_ref, s_ref, u_ref, v_ref)):
        col_ref[a] = strips([ref[k] for k in range(LEVELS)])
    col_ref[4] = strips([kap_ref[...], dep_ref[...].astype(F32)])
    q = lax.axis_index("gx")
    dep = dep_ref[...]
    above = jnp.zeros((ROWS, LANES), F32)
    carry = jnp.zeros((ROWS, LANES), F32)
    for k in range(LEVELS):
        below = jnp.where(dep > k + 1, mix_ref[k], 0.0) if k < LEVELS - 1 else jnp.zeros((ROWS, LANES), F32)
        inv = 1.0 / ((1.0 + above + below) - above * carry)
        carry = below * inv
        inv_ref[k] = inv
        down_ref[k] = above * inv
        up_ref[k] = carry
        above = below
    src = src_ref[...]
    sky = sky_ref[...]
    row, col = src >> 7, src & 127
    table = area_ref[...]
    table = jnp.broadcast_to(jnp.concatenate([table, table], axis=1), (16, LANES))
    area = jnp.take_along_axis(table, ptr_ref[...], axis=1)
    rise = (sky >> 11) - (row >> 1)
    east = ((sky & 2047) - (q * 64 + (col >> 1))) & 2047
    kind = jnp.where(east == 1, 1, jnp.where(rise == 1, 2, jnp.where(rise == -1, 3, 0)))
    high = kind * 8 + row
    part = []
    rest = area
    for _ in range(3):
        piece = rest.astype(BF16).astype(F32)
        part.append(piece)
        rest = rest - piece
    sums = jnp.zeros((96, LANES), F32)
    for i in range(0, 16, 2):
        left, right = [], []
        for j in (i, i + 1):
            hit = jnp.broadcast_to(high[j : j + 1], (32, LANES)) == iota((32, LANES), 0)
            left.append(
                jnp.concatenate(
                    [jnp.where(hit, jnp.broadcast_to(p[j : j + 1], (32, LANES)), 0.0) for p in part], axis=0
                )
            )
            same = jnp.broadcast_to(col[j : j + 1], (LANES, LANES)) == iota((LANES, LANES), 0)
            right.append(jnp.where(same, 1.0, 0.0))
        sums = sums + lax.dot_general(
            jnp.concatenate(left, axis=1).astype(BF16),
            jnp.concatenate(right, axis=1).astype(BF16),
            (((1,), (1,)), ((), ())),
            preferred_element_type=F32,
        )
    sums = sums[0:32] + sums[32:64] + sums[64:96]
    wet = jnp.where(dep > 0, 1.0, 0.0)
    for m in range(4):
        weight_ref[m] = sums[m * 8 : m * 8 + 8] * wet
    lane = iota((ROWS, LANES), 1)
    sub = iota((ROWS, LANES), 0)
    nextq = (q + 1) & 31
    own, hot = [], []
    outside = jnp.full((ROWS, LANES), -1, jnp.int32)
    for r in range(4):
        line = jnp.broadcast_to(place_ref[pl.ds(r * 16 + (q >> 1), 1), :], (ROWS, LANES))
        place = jnp.take_along_axis(line, (lane >> 1) + 64 * (q & 1), axis=1)
        own.append(place)
        hot.append(jnp.where(jnp.broadcast_to(seat(place[0:1]), (32, LANES)) == iota((32, LANES), 0), 1.0, 0.0))
        line = jnp.broadcast_to(place_ref[pl.ds(r * 16 + (nextq >> 1), 1), :], (ROWS, LANES))
        place = jnp.take_along_axis(line, (lane & 0) + 64 * (nextq & 1), axis=1)
        outside = jnp.where((lane >> 1) == r, place, outside)
    line = jnp.where(outside[0:1] < 0, -1, seat(outside[0:1]))
    hot.append(jnp.where(jnp.broadcast_to(line, (32, LANES)) == iota((32, LANES), 0), 1.0, 0.0))
    owner = jnp.concatenate(hot, axis=1).astype(BF16)
    owner_ref[...] = owner
    stacked = jnp.concatenate(hot[:4], axis=0).astype(BF16)
    low, this = iota((LANES, LANES), 0), iota((LANES, LANES), 1)
    single = (low & 1) == 0
    before = jnp.where(single & ((low >> 1) < (this >> 1)), 1.0, 0.0).astype(BF16)
    every = jnp.where(single, 1.0, 0.0).astype(BF16)
    ahead = jnp.dot(stacked, before, preferred_element_type=F32)
    whole = jnp.dot(stacked, every, preferred_element_type=F32)
    carried = jnp.zeros((32, LANES), F32)
    slots = []
    for r in range(4):
        count = ahead[r * 32 : r * 32 + 32] + carried
        carried = carried + whole[r * 32 : r * 32 + 32]
        rank = jnp.sum(hot[r] * count, axis=0, keepdims=True).astype(jnp.int32)
        chosen = jnp.where(jnp.broadcast_to(rank, (ROWS, LANES)) == sub, 1.0, 0.0)
        rank_ref[r] = chosen
        slots.append(jnp.where((lane & 1) == 0, chosen * (own[r] & 255).astype(F32), 0.0))
    slots.append(jnp.zeros((ROWS, LANES), F32))
    main = jnp.concatenate(slots, axis=1)
    extra = jnp.where(lane == 2 * sub, (outside & 255).astype(F32), 0.0)
    extra = jnp.where(sub < 4, extra, 0.0)
    extra = jnp.concatenate([jnp.zeros((ROWS, 4 * LANES), F32), extra], axis=1)
    lines = jnp.concatenate(
        [jnp.zeros((24, 5 * LANES), F32), main, extra, jnp.zeros((88, 5 * LANES), F32)], axis=0
    ).astype(BF16)
    slot_ref[...] = lax.dot_general(owner, lines, (((1,), (1,)), ((), ())), preferred_element_type=F32)


def main_kernel(
    t_ref, s_ref, u_ref, v_ref, kap_ref, dep_ref, first_ref, second_ref, two_ref, one_ref,
    inv_ref, down_ref, up_ref, weight_ref, owner_ref, rank_ref, slot_ref,
    tout_ref, sout_ref, send_ref, strip_ref, face_ref,
):
    shape = (ROWS, LANES)
    lane, sub = iota(shape, 1), iota(shape, 0)
    lane_first, lane_last = lane == 0, lane == LANES - 1
    row_first, row_last = sub == 0, sub == ROWS - 1
    mask = row_mask(lax.axis_index("gy") & 1)

    def ring(x, y, shift, axis, edge):
        rx, ry = pltpu.roll(x, shift, axis), pltpu.roll(y, shift, axis)
        return jnp.where(edge, ry, rx), jnp.where(edge, rx, ry)

    def east(f):
        a, b = ring(f[0], f[1], LANES - 1, 1, lane_last)
        h, g = ring(f[2], f[3], LANES - 1, 1, lane_last)
        return a, b, h, g

    def west(f):
        a, b = ring(f[0], f[1], 1, 1, lane_first)
        h, g = ring(f[2], f[3], 1, 1, lane_first)
        return a, b, h, g

    def north(f):
        a, h = ring(f[0], f[2], ROWS - 1, 0, row_last)
        b, g = ring(f[1], f[3], ROWS - 1, 0, row_last)
        return a, b, h, g

    def south(f):
        a, h = ring(f[0], f[2], 1, 0, row_first)
        b, g = ring(f[1], f[3], 1, 0, row_first)
        return a, b, h, g

    def pair(i):
        return unpair(i, mask, one_ref, two_ref)

    side = side_columns(first_ref, second_ref)
    corner = side[5:]
    for i in range(5):
        strip_ref[0, i] = side[i]
        strip_ref[1, i] = corner[i]

    def field(local, plane, k, outer):
        shift = (2 * LANES - 8 * k - 4) % LANES if isinstance(k, int) else (2 * LANES - 4) - 8 * k
        strips = [pltpu.roll(strip_ref[i, plane], shift, 1) for i in range(2)]
        return local, strips[0], outer, strips[1]

    outer_kap, outer_dep = pair(32)
    kap = field(kap_ref[...], 4, 0, outer_kap)
    dep = field(dep_ref[...].astype(F32), 4, 1, outer_dep)
    faces = (
        [0.5 * (x + y) for x, y in zip(kap, east(kap))],
        [0.5 * (x + y) for x, y in zip(kap, north(kap))],
        [jnp.minimum(x, y) for x, y in zip(dep, east(dep))],
        [jnp.minimum(x, y) for x, y in zip(dep, north(dep))],
    )
    for i, face in enumerate(faces):
        for j in range(4):
            face_ref[i, j] = face[j]

    def level(k, outer):
        u = field(u_ref[k], 2, k, outer[2])
        v = field(v_ref[k], 3, k, outer[3])
        level_f = lax.convert_element_type(k, F32)

        def face(rate, which):
            here, there = [], []
            for i, r in enumerate(rate):
                c = face_ref[which, i]
                wet = face_ref[which + 2, i] > level_f
                here.append(jnp.where(wet, jnp.maximum(r, 0.0) + c, 0.0))
                there.append(jnp.where(wet, c - jnp.minimum(r, 0.0), 0.0))
            return here, there

        here_e, from_e = face(u, 0)
        here_n, from_n = face(v, 1)
        from_w = west(here_e)
        from_s = south(here_n)
        back_e = west(from_e)
        back_n = south(from_n)
        keep = [1.0 - ((a + b) + (c + d)) for a, b, c, d in zip(here_e, back_e, here_n, back_n)]
        cells = [field(ref[k], i, k, outer[i]) for i, ref in enumerate((t_ref, s_ref))]
        for step in range(NSUB):
            for i, c in enumerate(cells):
                around = zip(keep, c, from_e, east(c), from_w, west(c), from_n, north(c), from_s, south(c))
                new = []
                for c0, x, ce, xe, cw, xw, cn, xn, cs, xs in around:
                    new.append((c0 * x + (ce * xe + cw * xw)) + (cn * xn + cs * xs))
                    if step == NSUB - 1:
                        break
                cells[i] = new
        tout_ref[k] = cells[0][0]
        sout_ref[k] = cells[1][0]

    def two_levels(k, nothing):
        pairs = [pair(a * 8 + k) for a in range(4)]
        level(k, [p[0] for p in pairs])
        level(k + 8, [p[1] for p in pairs])
        return nothing

    lax.fori_loop(0, 8, two_levels, 0, unroll=2)

    tops = []
    for out_ref in (tout_ref, sout_ref):
        value = out_ref[0] * inv_ref[0]
        values = [value]
        for k in range(1, LEVELS):
            value = out_ref[k] * inv_ref[k] + down_ref[k] * value
            values.append(value)
        out_ref[LEVELS - 1] = value
        for k in range(LEVELS - 2, -1, -1):
            value = values[k] + up_ref[k] * value
            out_ref[k] = value
        tops.append(value)

    lines, extra = [], jnp.zeros(shape, F32)
    for t, top in enumerate(tops):
        moved = pltpu.roll(weight_ref[1] * top, 2, 1)
        beyond = lane < 2
        total = weight_ref[0] * top + jnp.where(beyond, 0.0, moved)
        total = total + pltpu.roll(weight_ref[2] * top, 2, 0)
        total = total + pltpu.roll(weight_ref[3] * top, ROWS - 2, 0)
        total = total + pltpu.roll(total, ROWS - 1, 0)
        moved = jnp.where(beyond, moved, 0.0)
        moved = moved + pltpu.roll(moved, ROWS - 1, 0)
        blocks = []
        for r in range(4):
            blocks.append(rank_ref[r] * jnp.broadcast_to(total[2 * r : 2 * r + 1], shape))
            line = jnp.broadcast_to(moved[2 * r : 2 * r + 1], shape)
            line = pltpu.roll(line, 2 * r, 1) if r else line
            extra = jnp.where(sub == 4 * t + r, line, extra)
        blocks.append(jnp.zeros(shape, F32))
        lines.append(jnp.concatenate(blocks, axis=1))
    lines.append(jnp.concatenate([jnp.zeros((ROWS, 4 * LANES), F32), extra], axis=1))
    rest = jnp.concatenate(lines, axis=0)
    owner = owner_ref[...]
    send = jnp.zeros((32, 24), F32)
    for _ in range(3):
        piece = rest.astype(BF16)
        rest = rest - piece.astype(F32)
        send = send + lax.dot_general(owner, piece, (((1,), (1,)), ((), ())), preferred_element_type=F32)
    send_ref[...] = slot_ref[...]
    send_ref[:, 0:24] = send


def owner_kernel(got_ref, air_ref):
    got = got_ref[...]
    shape = (32, LANES)
    lane = iota(shape, 1).astype(F32)
    sums = [[jnp.zeros(shape, F32) for _ in range(2)] for _ in range(2)]
    for j in range(12):
        first, second, place = (j, 8 + j, 24 + j) if j < 8 else (8 + j, 12 + j, 24 + j)
        slot = jnp.broadcast_to(got[:, place : place + 1], shape)
        terms = [jnp.broadcast_to(got[:, first : first + 1], shape), jnp.broadcast_to(got[:, second : second + 1], shape)]
        for half in range(2):
            hit = slot == lane + float(half * LANES)
            for t in range(2):
                sums[t][half] = sums[t][half] + jnp.where(hit, terms[t], 0.0)
    for t in range(2):
        for half in range(2):
            air_ref[t, :, half * LANES : half * LANES + LANES] = jnp.sum(sums[t][half], axis=0, keepdims=True)


VMEM = pl.BlockSpec(memory_space=pltpu.VMEM)


def call(kernel, name, outs, n_in, flops, **kw):
    kw.setdefault("in_specs", [VMEM] * n_in)
    kw.setdefault("compiler_params", pltpu.CompilerParams(vmem_limit_bytes=16 << 20))
    return pl.pallas_call(
        kernel,
        name=name,
        out_shape=tuple(jax.ShapeDtypeStruct(s, d) for s, d in outs),
        out_specs=tuple([VMEM] * len(outs)),
        cost_estimate=pl.CostEstimate(flops=flops, bytes_accessed=1 << 20, transcendentals=0),
        **kw,
    )


def shards(
    thermal_anomaly,
    saltiness_anomaly,
    zonal_volume_rate,
    meridional_volume_rate,
    sideways_diffusivity_factor,
    stratum_interface_mixing,
    flooded_strata,
    patch_sea_source,
    patch_sky_target,
    patch_measure_pointer,
    patch_measures,
    holder_ordering,
):
    nx, ny = lax.axis_size("gx"), lax.axis_size("gy")
    fields = (
        thermal_anomaly,
        saltiness_anomaly,
        zonal_volume_rate,
        meridional_volume_rate,
        sideways_diffusivity_factor,
        flooded_strata,
    )
    plane = (ROWS, LANES)
    one, two, *held = call(
        rows_kernel,
        "rows",
        [((33,) + plane, F32)] * 2 + [(x.shape, x.dtype) for x in fields],
        6,
        1 << 18,
        in_specs=[pl.BlockSpec(memory_space=pltpu.HBM)] * 6,
        scratch_shapes=[pltpu.SemaphoreType.DMA((6,))],
    )(*[pltpu.with_memory_space_constraint(x, pltpu.HBM) for x in fields])

    def swap(x, axis, count, start, wrap):
        pairs = []
        for i in range(start, count, 2):
            if i + 1 < count or wrap:
                pairs += [(i, (i + 1) % count), ((i + 1) % count, i)]
        return lax.ppermute(x, axis, pairs)

    two = swap(two, "gy", ny, 1, False)
    one = swap(one, "gy", ny, 0, False)
    column3 = ((LEVELS,) + plane, F32)
    *prepared, column = call(
        prep_kernel,
        "prep",
        [
            column3,
            column3,
            column3,
            ((4,) + plane, F32),
            ((32, 5 * LANES), BF16),
            ((4,) + plane, F32),
            ((32, LANES), F32),
            ((5,) + plane, F32),
        ],
        12,
        1 << 26,
    )(
        patch_sea_source.reshape(16, LANES),
        patch_sky_target.reshape(16, LANES),
        patch_measure_pointer.reshape(16, LANES),
        patch_measures.reshape(1, 64),
        holder_ordering.reshape(64, LANES),
        stratum_interface_mixing,
        *held,
    )
    (column,) = call(columns_kernel, "columns", [((10,) + plane, F32)], 3, 1 << 16)(column, two, one)
    second = swap(column, "gx", nx, 1, True)
    first = swap(column, "gx", nx, 0, True)
    temperature, salinity, send = call(
        main_kernel,
        "main",
        [column3, column3, ((32, LANES), F32)],
        17,
        1 << 24,
        scratch_shapes=[pltpu.VMEM((2, 5) + plane, F32), pltpu.VMEM((4, 4) + plane, F32)],
    )(*held, first, second, two, one, *prepared)
    order = [[(i + LEAD) % nx for i in range(nx)]]
    got = lax.all_to_all(send.reshape(nx, 1, LANES), "gx", 0, 0, tiled=True, axis_index_groups=order)
    (air,) = call(owner_kernel, "owner", [((2, 1, 256), F32)], 1, 1 << 20)(got.reshape(nx, LANES))
    return temperature, salinity, air


def solution(mesh):
    placed = (
        P(None, "gy", "gx"),
        P(None, "gy", "gx"),
        P(None, "gy", "gx"),
        P(None, "gy", "gx"),
        P("gy", "gx"),
        P(None, "gy", "gx"),
        P("gy", "gx"),
        P("gy", "gx"),
        P("gy", "gx"),
        P("gy", "gx"),
        P(),
        P("gy", None),
    )
    return jax.shard_map(
        shards,
        mesh=mesh,
        in_specs=placed,
        out_specs=(P(None, "gy", "gx"), P(None, "gy", "gx"), P(None, "gy", "gx")),
        check_vma=False,
    )
```

```python
import jax
import jax.numpy as jnp
from jax import lax
from jax.experimental import pallas as pl
from jax.experimental.pallas import tpu as pltpu
from jax.sharding import PartitionSpec as P

NSUB = 4
LEVELS = 16
ROWS = 8
LANES = 128
F32 = jnp.float32
BF16 = jnp.bfloat16


LEAD = 18


def seat(place):
    return ((place >> 8) - LEAD) & 31


def iota(shape, dim):
    return lax.broadcasted_iota(jnp.int32, shape, dim)


def row_mask(parity):
    return (((iota((ROWS, LANES), 0) >> 2) + parity) & 1) == 0


def strips(planes):
    slot = iota((ROWS, LANES), 1) >> 3
    strip = jnp.zeros((ROWS, LANES), F32)
    for k, plane in enumerate(planes):
        strip = jnp.where(slot == k, pltpu.roll(plane, (8 * k + 4) % LANES, 1), strip)
    return strip


def rows_kernel(*refs):
    sources, (one_ref, two_ref), held, sem = refs[:6], refs[6:8], refs[8:14], refs[14]
    copies = [pltpu.make_async_copy(x, y, sem.at[i]) for i, (x, y) in enumerate(zip(sources, held))]
    for copy in copies:
        copy.start()
    mask = row_mask(lax.axis_index("gy") & 1)

    def put(i, here, there):
        there = pltpu.roll(there, 4, 0)
        one_ref[i] = jnp.where(mask, there, here)
        two_ref[i] = jnp.where(mask, here, there)

    for a in range(4):
        copies[a].wait()
        for k in range(8):
            put(a * 8 + k, held[a][k], held[a][k + 8])
    copies[4].wait()
    copies[5].wait()
    put(32, held[4][...], held[5][...].astype(F32))


def unpair(i, mask, one_ref, two_ref):
    x, y = one_ref[i], two_ref[i]
    return jnp.where(mask, x, y), pltpu.roll(jnp.where(mask, y, x), 4, 0)


def columns_kernel(local_ref, two_ref, one_ref, col_ref):
    mask = row_mask(lax.axis_index("gy") & 1)
    for a in range(4):
        pairs = [unpair(a * 8 + k, mask, one_ref, two_ref) for k in range(8)]
        col_ref[a] = local_ref[a]
        col_ref[5 + a] = strips([x[0] for x in pairs] + [x[1] for x in pairs])
    col_ref[4] = local_ref[4]
    col_ref[9] = strips(unpair(32, mask, one_ref, two_ref))


def side_columns(first_ref, second_ref):
    parity = lax.axis_index("gx") & 1
    mask = (((iota((ROWS, LANES), 1) >> 2) + parity) & 1) == 0
    return [jnp.where(mask, second_ref[a], first_ref[a]) for a in range(10)]


def prep_kernel(
    src_ref, sky_ref, ptr_ref, area_ref, place_ref, mix_ref, t_ref, s_ref, u_ref, v_ref, kap_ref, dep_ref,
    inv_ref, down_ref, up_ref, weight_ref, owner_ref, rank_ref, slot_ref, col_ref,
):
    for a, ref in enumerate((t_ref, s_ref, u_ref, v_ref)):
        col_ref[a] = strips([ref[k] for k in range(LEVELS)])
    col_ref[4] = strips([kap_ref[...], dep_ref[...].astype(F32)])
    q = lax.axis_index("gx")
    dep = dep_ref[...]
    above = jnp.zeros((ROWS, LANES), F32)
    carry = jnp.zeros((ROWS, LANES), F32)
    for k in range(LEVELS):
        below = jnp.where(dep > k + 1, mix_ref[k], 0.0) if k < LEVELS - 1 else jnp.zeros((ROWS, LANES), F32)
        inv = 1.0 / ((1.0 + above + below) - above * carry)
        carry = below * inv
        inv_ref[k] = inv
        down_ref[k] = above * inv
        up_ref[k] = carry
        above = below
    src = src_ref[...]
    sky = sky_ref[...]
    row, col = src >> 7, src & 127
    table = area_ref[...]
    table = jnp.broadcast_to(jnp.concatenate([table, table], axis=1), (16, LANES))
    area = jnp.take_along_axis(table, ptr_ref[...], axis=1)
    rise = (sky >> 11) - (row >> 1)
    east = ((sky & 2047) - (q * 64 + (col >> 1))) & 2047
    kind = jnp.where(east == 1, 1, jnp.where(rise == 1, 2, jnp.where(rise == -1, 3, 0)))
    high = kind * 8 + row
    part = []
    rest = area
    for _ in range(3):
        piece = rest.astype(BF16).astype(F32)
        part.append(piece)
        rest = rest - piece
    sums = jnp.zeros((96, LANES), F32)
    for i in range(0, 16, 2):
        left, right = [], []
        for j in (i, i + 1):
            hit = jnp.broadcast_to(high[j : j + 1], (32, LANES)) == iota((32, LANES), 0)
            left.append(
                jnp.concatenate(
                    [jnp.where(hit, jnp.broadcast_to(p[j : j + 1], (32, LANES)), 0.0) for p in part], axis=0
                )
            )
            same = jnp.broadcast_to(col[j : j + 1], (LANES, LANES)) == iota((LANES, LANES), 0)
            right.append(jnp.where(same, 1.0, 0.0))
        sums = sums + lax.dot_general(
            jnp.concatenate(left, axis=1).astype(BF16),
            jnp.concatenate(right, axis=1).astype(BF16),
            (((1,), (1,)), ((), ())),
            preferred_element_type=F32,
        )
    sums = sums[0:32] + sums[32:64] + sums[64:96]
    wet = jnp.where(dep > 0, 1.0, 0.0)
    for m in range(4):
        weight_ref[m] = sums[m * 8 : m * 8 + 8] * wet
    lane = iota((ROWS, LANES), 1)
    sub = iota((ROWS, LANES), 0)
    nextq = (q + 1) & 31
    own, hot = [], []
    outside = jnp.full((ROWS, LANES), -1, jnp.int32)
    for r in range(4):
        line = jnp.broadcast_to(place_ref[pl.ds(r * 16 + (q >> 1), 1), :], (ROWS, LANES))
        place = jnp.take_along_axis(line, (lane >> 1) + 64 * (q & 1), axis=1)
        own.append(place)
        hot.append(jnp.where(jnp.broadcast_to(seat(place[0:1]), (32, LANES)) == iota((32, LANES), 0), 1.0, 0.0))
        line = jnp.broadcast_to(place_ref[pl.ds(r * 16 + (nextq >> 1), 1), :], (ROWS, LANES))
        place = jnp.take_along_axis(line, (lane & 0) + 64 * (nextq & 1), axis=1)
        outside = jnp.where((lane >> 1) == r, place, outside)
    line = jnp.where(outside[0:1] < 0, -1, seat(outside[0:1]))
    hot.append(jnp.where(jnp.broadcast_to(line, (32, LANES)) == iota((32, LANES), 0), 1.0, 0.0))
    owner = jnp.concatenate(hot, axis=1).astype(BF16)
    owner_ref[...] = owner
    stacked = jnp.concatenate(hot[:4], axis=0).astype(BF16)
    low, this = iota((LANES, LANES), 0), iota((LANES, LANES), 1)
    single = (low & 1) == 0
    before = jnp.where(single & ((low >> 1) < (this >> 1)), 1.0, 0.0).astype(BF16)
    every = jnp.where(single, 1.0, 0.0).astype(BF16)
    ahead = jnp.dot(stacked, before, preferred_element_type=F32)
    whole = jnp.dot(stacked, every, preferred_element_type=F32)
    carried = jnp.zeros((32, LANES), F32)
    slots = []
    for r in range(4):
        count = ahead[r * 32 : r * 32 + 32] + carried
        carried = carried + whole[r * 32 : r * 32 + 32]
        rank = jnp.sum(hot[r] * count, axis=0, keepdims=True).astype(jnp.int32)
        chosen = jnp.where(jnp.broadcast_to(rank, (ROWS, LANES)) == sub, 1.0, 0.0)
        rank_ref[r] = chosen
        slots.append(jnp.where((lane & 1) == 0, chosen * (own[r] & 255).astype(F32), 0.0))
    slots.append(jnp.zeros((ROWS, LANES), F32))
    main = jnp.concatenate(slots, axis=1)
    extra = jnp.where(lane == 2 * sub, (outside & 255).astype(F32), 0.0)
    extra = jnp.where(sub < 4, extra, 0.0)
    extra = jnp.concatenate([jnp.zeros((ROWS, 4 * LANES), F32), extra], axis=1)
    lines = jnp.concatenate(
        [jnp.zeros((24, 5 * LANES), F32), main, extra, jnp.zeros((88, 5 * LANES), F32)], axis=0
    ).astype(BF16)
    slot_ref[...] = lax.dot_general(owner, lines, (((1,), (1,)), ((), ())), preferred_element_type=F32)


def main_kernel(
    t_ref, s_ref, u_ref, v_ref, kap_ref, dep_ref, first_ref, second_ref, two_ref, one_ref,
    inv_ref, down_ref, up_ref, weight_ref, owner_ref, rank_ref, slot_ref,
    tout_ref, sout_ref, send_ref, strip_ref, face_ref,
):
    shape = (ROWS, LANES)
    lane, sub = iota(shape, 1), iota(shape, 0)
    lane_first, lane_last = lane == 0, lane == LANES - 1
    row_first, row_last = sub == 0, sub == ROWS - 1
    mask = row_mask(lax.axis_index("gy") & 1)

    def ring(x, y, shift, axis, edge):
        rx, ry = pltpu.roll(x, shift, axis), pltpu.roll(y, shift, axis)
        return jnp.where(edge, ry, rx), jnp.where(edge, rx, ry)

    def east(f):
        a, b = ring(f[0], f[1], LANES - 1, 1, lane_last)
        h, g = ring(f[2], f[3], LANES - 1, 1, lane_last)
        return a, b, h, g

    def west(f):
        a, b = ring(f[0], f[1], 1, 1, lane_first)
        h, g = ring(f[2], f[3], 1, 1, lane_first)
        return a, b, h, g

    def north(f):
        a, h = ring(f[0], f[2], ROWS - 1, 0, row_last)
        b, g = ring(f[1], f[3], ROWS - 1, 0, row_last)
        return a, b, h, g

    def south(f):
        a, h = ring(f[0], f[2], 1, 0, row_first)
        b, g = ring(f[1], f[3], 1, 0, row_first)
        return a, b, h, g

    def pair(i):
        return unpair(i, mask, one_ref, two_ref)

    side = side_columns(first_ref, second_ref)
    corner = side[5:]
    for i in range(5):
        strip_ref[0, i] = side[i]
        strip_ref[1, i] = corner[i]

    def field(local, plane, k, outer):
        shift = (2 * LANES - 8 * k - 4) % LANES if isinstance(k, int) else (2 * LANES - 4) - 8 * k
        strips = [pltpu.roll(strip_ref[i, plane], shift, 1) for i in range(2)]
        return local, strips[0], outer, strips[1]

    outer_kap, outer_dep = pair(32)
    kap = field(kap_ref[...], 4, 0, outer_kap)
    dep = field(dep_ref[...].astype(F32), 4, 1, outer_dep)
    faces = (
        [0.5 * (x + y) for x, y in zip(kap, east(kap))],
        [0.5 * (x + y) for x, y in zip(kap, north(kap))],
        [jnp.minimum(x, y) for x, y in zip(dep, east(dep))],
        [jnp.minimum(x, y) for x, y in zip(dep, north(dep))],
    )
    for i, face in enumerate(faces):
        for j in range(4):
            face_ref[i, j] = face[j]

    def level(k, outer):
        u = field(u_ref[k], 2, k, outer[2])
        v = field(v_ref[k], 3, k, outer[3])
        level_f = lax.convert_element_type(k, F32)

        def face(rate, which):
            here, there = [], []
            for i, r in enumerate(rate):
                c = face_ref[which, i]
                wet = face_ref[which + 2, i] > level_f
                here.append(jnp.where(wet, jnp.maximum(r, 0.0) + c, 0.0))
                there.append(jnp.where(wet, c - jnp.minimum(r, 0.0), 0.0))
            return here, there

        here_e, from_e = face(u, 0)
        here_n, from_n = face(v, 1)
        from_w = west(here_e)
        from_s = south(here_n)
        back_e = west(from_e)
        back_n = south(from_n)
        keep = [1.0 - ((a + b) + (c + d)) for a, b, c, d in zip(here_e, back_e, here_n, back_n)]
        cells = [field(ref[k], i, k, outer[i]) for i, ref in enumerate((t_ref, s_ref))]
        for step in range(NSUB):
            for i, c in enumerate(cells):
                around = zip(keep, c, from_e, east(c), from_w, west(c), from_n, north(c), from_s, south(c))
                new = []
                for c0, x, ce, xe, cw, xw, cn, xn, cs, xs in around:
                    new.append((c0 * x + (ce * xe + cw * xw)) + (cn * xn + cs * xs))
                    if step == NSUB - 1:
                        break
                cells[i] = new
        tout_ref[k] = cells[0][0]
        sout_ref[k] = cells[1][0]

    def two_levels(k, nothing):
        pairs = [pair(a * 8 + k) for a in range(4)]
        level(k, [p[0] for p in pairs])
        level(k + 8, [p[1] for p in pairs])
        return nothing

    lax.fori_loop(0, 8, two_levels, 0, unroll=2)

    tops = []
    for out_ref in (tout_ref, sout_ref):
        value = out_ref[0] * inv_ref[0]
        values = [value]
        for k in range(1, LEVELS):
            value = out_ref[k] * inv_ref[k] + down_ref[k] * value
            values.append(value)
        out_ref[LEVELS - 1] = value
        for k in range(LEVELS - 2, -1, -1):
            value = values[k] + up_ref[k] * value
            out_ref[k] = value
        tops.append(value)

    lines, extra = [], jnp.zeros(shape, F32)
    for t, top in enumerate(tops):
        moved = pltpu.roll(weight_ref[1] * top, 2, 1)
        beyond = lane < 2
        total = weight_ref[0] * top + jnp.where(beyond, 0.0, moved)
        total = total + pltpu.roll(weight_ref[2] * top, 2, 0)
        total = total + pltpu.roll(weight_ref[3] * top, ROWS - 2, 0)
        total = total + pltpu.roll(total, ROWS - 1, 0)
        moved = jnp.where(beyond, moved, 0.0)
        moved = moved + pltpu.roll(moved, ROWS - 1, 0)
        blocks = []
        for r in range(4):
            blocks.append(rank_ref[r] * jnp.broadcast_to(total[2 * r : 2 * r + 1], shape))
            line = jnp.broadcast_to(moved[2 * r : 2 * r + 1], shape)
            line = pltpu.roll(line, 2 * r, 1) if r else line
            extra = jnp.where(sub == 4 * t + r, line, extra)
        blocks.append(jnp.zeros(shape, F32))
        lines.append(jnp.concatenate(blocks, axis=1))
    lines.append(jnp.concatenate([jnp.zeros((ROWS, 4 * LANES), F32), extra], axis=1))
    rest = jnp.concatenate(lines, axis=0)
    owner = owner_ref[...]
    send = jnp.zeros((32, 24), F32)
    for _ in range(3):
        piece = rest.astype(BF16)
        rest = rest - piece.astype(F32)
        send = send + lax.dot_general(owner, piece, (((1,), (1,)), ((), ())), preferred_element_type=F32)
    send_ref[...] = slot_ref[...]
    send_ref[:, 0:24] = send


def owner_kernel(got_ref, air_ref):
    got = got_ref[...]
    shape = (32, LANES)
    lane = iota(shape, 1).astype(F32)
    sums = [[jnp.zeros(shape, F32) for _ in range(2)] for _ in range(2)]
    for j in range(12):
        first, second, place = (j, 8 + j, 24 + j) if j < 8 else (8 + j, 12 + j, 24 + j)
        slot = jnp.broadcast_to(got[:, place : place + 1], shape)
        terms = [jnp.broadcast_to(got[:, first : first + 1], shape), jnp.broadcast_to(got[:, second : second + 1], shape)]
        for half in range(2):
            hit = slot == lane + float(half * LANES)
            for t in range(2):
                sums[t][half] = sums[t][half] + jnp.where(hit, terms[t], 0.0)
    for t in range(2):
        for half in range(2):
            air_ref[t, :, half * LANES : half * LANES + LANES] = jnp.sum(sums[t][half], axis=0, keepdims=True)


VMEM = pl.BlockSpec(memory_space=pltpu.VMEM)


def call(kernel, name, outs, n_in, flops, **kw):
    kw.setdefault("in_specs", [VMEM] * n_in)
    kw.setdefault("compiler_params", pltpu.CompilerParams(vmem_limit_bytes=16 << 20))
    return pl.pallas_call(
        kernel,
        name=name,
        out_shape=tuple(jax.ShapeDtypeStruct(s, d) for s, d in outs),
        out_specs=tuple([VMEM] * len(outs)),
        cost_estimate=pl.CostEstimate(flops=flops, bytes_accessed=1 << 20, transcendentals=0),
        **kw,
    )


def shards(
    thermal_anomaly,
    saltiness_anomaly,
    zonal_volume_rate,
    meridional_volume_rate,
    sideways_diffusivity_factor,
    stratum_interface_mixing,
    flooded_strata,
    patch_sea_source,
    patch_sky_target,
    patch_measure_pointer,
    patch_measures,
    holder_ordering,
):
    nx, ny = lax.axis_size("gx"), lax.axis_size("gy")
    fields = (
        thermal_anomaly,
        saltiness_anomaly,
        zonal_volume_rate,
        meridional_volume_rate,
        sideways_diffusivity_factor,
        flooded_strata,
    )
    plane = (ROWS, LANES)
    one, two, *held = call(
        rows_kernel,
        "rows",
        [((33,) + plane, F32)] * 2 + [(x.shape, x.dtype) for x in fields],
        6,
        1 << 18,
        in_specs=[pl.BlockSpec(memory_space=pltpu.HBM)] * 6,
        scratch_shapes=[pltpu.SemaphoreType.DMA((6,))],
    )(*[pltpu.with_memory_space_constraint(x, pltpu.HBM) for x in fields])

    def swap(x, axis, count, start, wrap):
        pairs = []
        for i in range(start, count, 2):
            if i + 1 < count or wrap:
                pairs += [(i, (i + 1) % count), ((i + 1) % count, i)]
        return lax.ppermute(x, axis, pairs)

    two = swap(two, "gy", ny, 1, False)
    one = swap(one, "gy", ny, 0, False)
    column3 = ((LEVELS,) + plane, F32)
    *prepared, column = call(
        prep_kernel,
        "prep",
        [
            column3,
            column3,
            column3,
            ((4,) + plane, F32),
            ((32, 5 * LANES), BF16),
            ((4,) + plane, F32),
            ((32, LANES), F32),
            ((5,) + plane, F32),
        ],
        12,
        1 << 26,
    )(
        patch_sea_source.reshape(16, LANES),
        patch_sky_target.reshape(16, LANES),
        patch_measure_pointer.reshape(16, LANES),
        patch_measures.reshape(1, 64),
        holder_ordering.reshape(64, LANES),
        stratum_interface_mixing,
        *held,
    )
    (column,) = call(columns_kernel, "columns", [((10,) + plane, F32)], 3, 1 << 16)(column, two, one)
    second = swap(column, "gx", nx, 1, True)
    first = swap(column, "gx", nx, 0, True)
    temperature, salinity, send = call(
        main_kernel,
        "main",
        [column3, column3, ((32, LANES), F32)],
        17,
        1 << 24,
        scratch_shapes=[pltpu.VMEM((2, 5) + plane, F32), pltpu.VMEM((4, 4) + plane, F32)],
    )(*held, first, second, two, one, *prepared)
    order = [[(i + LEAD) % nx for i in range(nx)]]
    got = lax.all_to_all(send.reshape(nx, 1, LANES), "gx", 0, 0, tiled=True, axis_index_groups=order)
    (air,) = call(owner_kernel, "owner", [((2, 1, 256), F32)], 1, 1 << 20)(got.reshape(nx, LANES))
    return temperature, salinity, air


def solution(mesh):
    placed = (
        P(None, "gy", "gx"),
        P(None, "gy", "gx"),
        P(None, "gy", "gx"),
        P(None, "gy", "gx"),
        P("gy", "gx"),
        P(None, "gy", "gx"),
        P("gy", "gx"),
        P("gy", "gx"),
        P("gy", "gx"),
        P("gy", "gx"),
        P(),
        P("gy", None),
    )
    return jax.shard_map(
        shards,
        mesh=mesh,
        in_specs=placed,
        out_specs=(P(None, "gy", "gx"), P(None, "gy", "gx"), P(None, "gy", "gx")),
        check_vma=False,
    )
```

```python
import jax
import jax.numpy as jnp
from jax import lax
from jax.experimental import pallas as pl
from jax.experimental.pallas import tpu as pltpu
from jax.sharding import PartitionSpec as P

NSUB = 4
LEVELS = 16
ROWS = 8
LANES = 128
F32 = jnp.float32
BF16 = jnp.bfloat16


LEAD = 17


def seat(place):
    return ((place >> 8) - LEAD) & 31


def iota(shape, dim):
    return lax.broadcasted_iota(jnp.int32, shape, dim)


def row_mask(parity):
    return (((iota((ROWS, LANES), 0) >> 2) + parity) & 1) == 0


def strips(planes):
    slot = iota((ROWS, LANES), 1) >> 3
    strip = jnp.zeros((ROWS, LANES), F32)
    for k, plane in enumerate(planes):
        strip = jnp.where(slot == k, pltpu.roll(plane, (8 * k + 4) % LANES, 1), strip)
    return strip


def rows_kernel(*refs):
    sources, (one_ref, two_ref), held, sem = refs[:6], refs[6:8], refs[8:14], refs[14]
    copies = [pltpu.make_async_copy(x, y, sem.at[i]) for i, (x, y) in enumerate(zip(sources, held))]
    for copy in copies:
        copy.start()
    mask = row_mask(lax.axis_index("gy") & 1)

    def put(i, here, there):
        there = pltpu.roll(there, 4, 0)
        one_ref[i] = jnp.where(mask, there, here)
        two_ref[i] = jnp.where(mask, here, there)

    for a in range(4):
        copies[a].wait()
        for k in range(8):
            put(a * 8 + k, held[a][k], held[a][k + 8])
    copies[4].wait()
    copies[5].wait()
    put(32, held[4][...], held[5][...].astype(F32))


def unpair(i, mask, one_ref, two_ref):
    x, y = one_ref[i], two_ref[i]
    return jnp.where(mask, x, y), pltpu.roll(jnp.where(mask, y, x), 4, 0)


def columns_kernel(local_ref, two_ref, one_ref, col_ref):
    mask = row_mask(lax.axis_index("gy") & 1)
    for a in range(4):
        pairs = [unpair(a * 8 + k, mask, one_ref, two_ref) for k in range(8)]
        col_ref[a] = local_ref[a]
        col_ref[5 + a] = strips([x[0] for x in pairs] + [x[1] for x in pairs])
    col_ref[4] = local_ref[4]
    col_ref[9] = strips(unpair(32, mask, one_ref, two_ref))


def side_columns(first_ref, second_ref):
    parity = lax.axis_index("gx") & 1
    mask = (((iota((ROWS, LANES), 1) >> 2) + parity) & 1) == 0
    return [jnp.where(mask, second_ref[a], first_ref[a]) for a in range(10)]


def prep_kernel(
    src_ref, sky_ref, ptr_ref, area_ref, place_ref, mix_ref, t_ref, s_ref, u_ref, v_ref, kap_ref, dep_ref,
    inv_ref, down_ref, up_ref, weight_ref, owner_ref, rank_ref, slot_ref, col_ref,
):
    for a, ref in enumerate((t_ref, s_ref, u_ref, v_ref)):
        col_ref[a] = strips([ref[k] for k in range(LEVELS)])
    col_ref[4] = strips([kap_ref[...], dep_ref[...].astype(F32)])
    q = lax.axis_index("gx")
    dep = dep_ref[...]
    above = jnp.zeros((ROWS, LANES), F32)
    carry = jnp.zeros((ROWS, LANES), F32)
    for k in range(LEVELS):
        below = jnp.where(dep > k + 1, mix_ref[k], 0.0) if k < LEVELS - 1 else jnp.zeros((ROWS, LANES), F32)
        inv = 1.0 / ((1.0 + above + below) - above * carry)
        carry = below * inv
        inv_ref[k] = inv
        down_ref[k] = above * inv
        up_ref[k] = carry
        above = below
    src = src_ref[...]
    sky = sky_ref[...]
    row, col = src >> 7, src & 127
    table = area_ref[...]
    table = jnp.broadcast_to(jnp.concatenate([table, table], axis=1), (16, LANES))
    area = jnp.take_along_axis(table, ptr_ref[...], axis=1)
    rise = (sky >> 11) - (row >> 1)
    east = ((sky & 2047) - (q * 64 + (col >> 1))) & 2047
    kind = jnp.where(east == 1, 1, jnp.where(rise == 1, 2, jnp.where(rise == -1, 3, 0)))
    high = kind * 8 + row
    part = []
    rest = area
    for _ in range(3):
        piece = rest.astype(BF16).astype(F32)
        part.append(piece)
        rest = rest - piece
    sums = jnp.zeros((96, LANES), F32)
    for i in range(0, 16, 2):
        left, right = [], []
        for j in (i, i + 1):
            hit = jnp.broadcast_to(high[j : j + 1], (32, LANES)) == iota((32, LANES), 0)
            left.append(
                jnp.concatenate(
                    [jnp.where(hit, jnp.broadcast_to(p[j : j + 1], (32, LANES)), 0.0) for p in part], axis=0
                )
            )
            same = jnp.broadcast_to(col[j : j + 1], (LANES, LANES)) == iota((LANES, LANES), 0)
            right.append(jnp.where(same, 1.0, 0.0))
        sums = sums + lax.dot_general(
            jnp.concatenate(left, axis=1).astype(BF16),
            jnp.concatenate(right, axis=1).astype(BF16),
            (((1,), (1,)), ((), ())),
            preferred_element_type=F32,
        )
    sums = sums[0:32] + sums[32:64] + sums[64:96]
    wet = jnp.where(dep > 0, 1.0, 0.0)
    for m in range(4):
        weight_ref[m] = sums[m * 8 : m * 8 + 8] * wet
    lane = iota((ROWS, LANES), 1)
    sub = iota((ROWS, LANES), 0)
    nextq = (q + 1) & 31
    own, hot = [], []
    outside = jnp.full((ROWS, LANES), -1, jnp.int32)
    for r in range(4):
        line = jnp.broadcast_to(place_ref[pl.ds(r * 16 + (q >> 1), 1), :], (ROWS, LANES))
        place = jnp.take_along_axis(line, (lane >> 1) + 64 * (q & 1), axis=1)
        own.append(place)
        hot.append(jnp.where(jnp.broadcast_to(seat(place[0:1]), (32, LANES)) == iota((32, LANES), 0), 1.0, 0.0))
        line = jnp.broadcast_to(place_ref[pl.ds(r * 16 + (nextq >> 1), 1), :], (ROWS, LANES))
        place = jnp.take_along_axis(line, (lane & 0) + 64 * (nextq & 1), axis=1)
        outside = jnp.where((lane >> 1) == r, place, outside)
    line = jnp.where(outside[0:1] < 0, -1, seat(outside[0:1]))
    hot.append(jnp.where(jnp.broadcast_to(line, (32, LANES)) == iota((32, LANES), 0), 1.0, 0.0))
    owner = jnp.concatenate(hot, axis=1).astype(BF16)
    owner_ref[...] = owner
    stacked = jnp.concatenate(hot[:4], axis=0).astype(BF16)
    low, this = iota((LANES, LANES), 0), iota((LANES, LANES), 1)
    single = (low & 1) == 0
    before = jnp.where(single & ((low >> 1) < (this >> 1)), 1.0, 0.0).astype(BF16)
    every = jnp.where(single, 1.0, 0.0).astype(BF16)
    ahead = jnp.dot(stacked, before, preferred_element_type=F32)
    whole = jnp.dot(stacked, every, preferred_element_type=F32)
    carried = jnp.zeros((32, LANES), F32)
    slots = []
    for r in range(4):
        count = ahead[r * 32 : r * 32 + 32] + carried
        carried = carried + whole[r * 32 : r * 32 + 32]
        rank = jnp.sum(hot[r] * count, axis=0, keepdims=True).astype(jnp.int32)
        chosen = jnp.where(jnp.broadcast_to(rank, (ROWS, LANES)) == sub, 1.0, 0.0)
        rank_ref[r] = chosen
        slots.append(jnp.where((lane & 1) == 0, chosen * (own[r] & 255).astype(F32), 0.0))
    slots.append(jnp.zeros((ROWS, LANES), F32))
    main = jnp.concatenate(slots, axis=1)
    extra = jnp.where(lane == 2 * sub, (outside & 255).astype(F32), 0.0)
    extra = jnp.where(sub < 4, extra, 0.0)
    extra = jnp.concatenate([jnp.zeros((ROWS, 4 * LANES), F32), extra], axis=1)
    lines = jnp.concatenate(
        [jnp.zeros((24, 5 * LANES), F32), main, extra, jnp.zeros((88, 5 * LANES), F32)], axis=0
    ).astype(BF16)
    slot_ref[...] = lax.dot_general(owner, lines, (((1,), (1,)), ((), ())), preferred_element_type=F32)


def main_kernel(
    t_ref, s_ref, u_ref, v_ref, kap_ref, dep_ref, first_ref, second_ref, two_ref, one_ref,
    inv_ref, down_ref, up_ref, weight_ref, owner_ref, rank_ref, slot_ref,
    tout_ref, sout_ref, send_ref, strip_ref, face_ref,
):
    shape = (ROWS, LANES)
    lane, sub = iota(shape, 1), iota(shape, 0)
    lane_first, lane_last = lane == 0, lane == LANES - 1
    row_first, row_last = sub == 0, sub == ROWS - 1
    mask = row_mask(lax.axis_index("gy") & 1)

    def ring(x, y, shift, axis, edge):
        rx, ry = pltpu.roll(x, shift, axis), pltpu.roll(y, shift, axis)
        return jnp.where(edge, ry, rx), jnp.where(edge, rx, ry)

    def east(f):
        a, b = ring(f[0], f[1], LANES - 1, 1, lane_last)
        h, g = ring(f[2], f[3], LANES - 1, 1, lane_last)
        return a, b, h, g

    def west(f):
        a, b = ring(f[0], f[1], 1, 1, lane_first)
        h, g = ring(f[2], f[3], 1, 1, lane_first)
        return a, b, h, g

    def north(f):
        a, h = ring(f[0], f[2], ROWS - 1, 0, row_last)
        b, g = ring(f[1], f[3], ROWS - 1, 0, row_last)
        return a, b, h, g

    def south(f):
        a, h = ring(f[0], f[2], 1, 0, row_first)
        b, g = ring(f[1], f[3], 1, 0, row_first)
        return a, b, h, g

    def pair(i):
        return unpair(i, mask, one_ref, two_ref)

    side = side_columns(first_ref, second_ref)
    corner = side[5:]
    for i in range(5):
        strip_ref[0, i] = side[i]
        strip_ref[1, i] = corner[i]

    def field(local, plane, k, outer):
        shift = (2 * LANES - 8 * k - 4) % LANES if isinstance(k, int) else (2 * LANES - 4) - 8 * k
        strips = [pltpu.roll(strip_ref[i, plane], shift, 1) for i in range(2)]
        return local, strips[0], outer, strips[1]

    outer_kap, outer_dep = pair(32)
    kap = field(kap_ref[...], 4, 0, outer_kap)
    dep = field(dep_ref[...].astype(F32), 4, 1, outer_dep)
    faces = (
        [0.5 * (x + y) for x, y in zip(kap, east(kap))],
        [0.5 * (x + y) for x, y in zip(kap, north(kap))],
        [jnp.minimum(x, y) for x, y in zip(dep, east(dep))],
        [jnp.minimum(x, y) for x, y in zip(dep, north(dep))],
    )
    for i, face in enumerate(faces):
        for j in range(4):
            face_ref[i, j] = face[j]

    def level(k, outer):
        u = field(u_ref[k], 2, k, outer[2])
        v = field(v_ref[k], 3, k, outer[3])
        level_f = lax.convert_element_type(k, F32)

        def face(rate, which):
            here, there = [], []
            for i, r in enumerate(rate):
                c = face_ref[which, i]
                wet = face_ref[which + 2, i] > level_f
                here.append(jnp.where(wet, jnp.maximum(r, 0.0) + c, 0.0))
                there.append(jnp.where(wet, c - jnp.minimum(r, 0.0), 0.0))
            return here, there

        here_e, from_e = face(u, 0)
        here_n, from_n = face(v, 1)
        from_w = west(here_e)
        from_s = south(here_n)
        back_e = west(from_e)
        back_n = south(from_n)
        keep = [1.0 - ((a + b) + (c + d)) for a, b, c, d in zip(here_e, back_e, here_n, back_n)]
        cells = [field(ref[k], i, k, outer[i]) for i, ref in enumerate((t_ref, s_ref))]
        for step in range(NSUB):
            for i, c in enumerate(cells):
                around = zip(keep, c, from_e, east(c), from_w, west(c), from_n, north(c), from_s, south(c))
                new = []
                for c0, x, ce, xe, cw, xw, cn, xn, cs, xs in around:
                    new.append((c0 * x + (ce * xe + cw * xw)) + (cn * xn + cs * xs))
                    if step == NSUB - 1:
                        break
                cells[i] = new
        tout_ref[k] = cells[0][0]
        sout_ref[k] = cells[1][0]

    def two_levels(k, nothing):
        pairs = [pair(a * 8 + k) for a in range(4)]
        level(k, [p[0] for p in pairs])
        level(k + 8, [p[1] for p in pairs])
        return nothing

    lax.fori_loop(0, 8, two_levels, 0, unroll=2)

    tops = []
    for out_ref in (tout_ref, sout_ref):
        value = out_ref[0] * inv_ref[0]
        values = [value]
        for k in range(1, LEVELS):
            value = out_ref[k] * inv_ref[k] + down_ref[k] * value
            values.append(value)
        out_ref[LEVELS - 1] = value
        for k in range(LEVELS - 2, -1, -1):
            value = values[k] + up_ref[k] * value
            out_ref[k] = value
        tops.append(value)

    lines, extra = [], jnp.zeros(shape, F32)
    for t, top in enumerate(tops):
        moved = pltpu.roll(weight_ref[1] * top, 2, 1)
        beyond = lane < 2
        total = weight_ref[0] * top + jnp.where(beyond, 0.0, moved)
        total = total + pltpu.roll(weight_ref[2] * top, 2, 0)
        total = total + pltpu.roll(weight_ref[3] * top, ROWS - 2, 0)
        total = total + pltpu.roll(total, ROWS - 1, 0)
        moved = jnp.where(beyond, moved, 0.0)
        moved = moved + pltpu.roll(moved, ROWS - 1, 0)
        blocks = []
        for r in range(4):
            blocks.append(rank_ref[r] * jnp.broadcast_to(total[2 * r : 2 * r + 1], shape))
            line = jnp.broadcast_to(moved[2 * r : 2 * r + 1], shape)
            line = pltpu.roll(line, 2 * r, 1) if r else line
            extra = jnp.where(sub == 4 * t + r, line, extra)
        blocks.append(jnp.zeros(shape, F32))
        lines.append(jnp.concatenate(blocks, axis=1))
    lines.append(jnp.concatenate([jnp.zeros((ROWS, 4 * LANES), F32), extra], axis=1))
    rest = jnp.concatenate(lines, axis=0)
    owner = owner_ref[...]
    send = jnp.zeros((32, 24), F32)
    for _ in range(3):
        piece = rest.astype(BF16)
        rest = rest - piece.astype(F32)
        send = send + lax.dot_general(owner, piece, (((1,), (1,)), ((), ())), preferred_element_type=F32)
    send_ref[...] = slot_ref[...]
    send_ref[:, 0:24] = send


def owner_kernel(got_ref, air_ref):
    got = got_ref[...]
    shape = (32, LANES)
    lane = iota(shape, 1).astype(F32)
    sums = [[jnp.zeros(shape, F32) for _ in range(2)] for _ in range(2)]
    for j in range(12):
        first, second, place = (j, 8 + j, 24 + j) if j < 8 else (8 + j, 12 + j, 24 + j)
        slot = jnp.broadcast_to(got[:, place : place + 1], shape)
        terms = [jnp.broadcast_to(got[:, first : first + 1], shape), jnp.broadcast_to(got[:, second : second + 1], shape)]
        for half in range(2):
            hit = slot == lane + float(half * LANES)
            for t in range(2):
                sums[t][half] = sums[t][half] + jnp.where(hit, terms[t], 0.0)
    for t in range(2):
        for half in range(2):
            air_ref[t, :, half * LANES : half * LANES + LANES] = jnp.sum(sums[t][half], axis=0, keepdims=True)


VMEM = pl.BlockSpec(memory_space=pltpu.VMEM)


def call(kernel, name, outs, n_in, flops, **kw):
    kw.setdefault("in_specs", [VMEM] * n_in)
    kw.setdefault("compiler_params", pltpu.CompilerParams(vmem_limit_bytes=16 << 20))
    return pl.pallas_call(
        kernel,
        name=name,
        out_shape=tuple(jax.ShapeDtypeStruct(s, d) for s, d in outs),
        out_specs=tuple([VMEM] * len(outs)),
        cost_estimate=pl.CostEstimate(flops=flops, bytes_accessed=1 << 20, transcendentals=0),
        **kw,
    )


def shards(
    thermal_anomaly,
    saltiness_anomaly,
    zonal_volume_rate,
    meridional_volume_rate,
    sideways_diffusivity_factor,
    stratum_interface_mixing,
    flooded_strata,
    patch_sea_source,
    patch_sky_target,
    patch_measure_pointer,
    patch_measures,
    holder_ordering,
):
    nx, ny = lax.axis_size("gx"), lax.axis_size("gy")
    fields = (
        thermal_anomaly,
        saltiness_anomaly,
        zonal_volume_rate,
        meridional_volume_rate,
        sideways_diffusivity_factor,
        flooded_strata,
    )
    plane = (ROWS, LANES)
    one, two, *held = call(
        rows_kernel,
        "rows",
        [((33,) + plane, F32)] * 2 + [(x.shape, x.dtype) for x in fields],
        6,
        1 << 18,
        in_specs=[pl.BlockSpec(memory_space=pltpu.HBM)] * 6,
        scratch_shapes=[pltpu.SemaphoreType.DMA((6,))],
    )(*[pltpu.with_memory_space_constraint(x, pltpu.HBM) for x in fields])

    def swap(x, axis, count, start, wrap):
        pairs = []
        for i in range(start, count, 2):
            if i + 1 < count or wrap:
                pairs += [(i, (i + 1) % count), ((i + 1) % count, i)]
        return lax.ppermute(x, axis, pairs)

    two = swap(two, "gy", ny, 1, False)
    one = swap(one, "gy", ny, 0, False)
    column3 = ((LEVELS,) + plane, F32)
    *prepared, column = call(
        prep_kernel,
        "prep",
        [
            column3,
            column3,
            column3,
            ((4,) + plane, F32),
            ((32, 5 * LANES), BF16),
            ((4,) + plane, F32),
            ((32, LANES), F32),
            ((5,) + plane, F32),
        ],
        12,
        1 << 26,
    )(
        patch_sea_source.reshape(16, LANES),
        patch_sky_target.reshape(16, LANES),
        patch_measure_pointer.reshape(16, LANES),
        patch_measures.reshape(1, 64),
        holder_ordering.reshape(64, LANES),
        stratum_interface_mixing,
        *held,
    )
    (column,) = call(columns_kernel, "columns", [((10,) + plane, F32)], 3, 1 << 16)(column, two, one)
    second = swap(column, "gx", nx, 1, True)
    first = swap(column, "gx", nx, 0, True)
    temperature, salinity, send = call(
        main_kernel,
        "main",
        [column3, column3, ((32, LANES), F32)],
        17,
        1 << 24,
        scratch_shapes=[pltpu.VMEM((2, 5) + plane, F32), pltpu.VMEM((4, 4) + plane, F32)],
    )(*held, first, second, two, one, *prepared)
    order = [[(i + LEAD) % nx for i in range(nx)]]
    got = lax.all_to_all(send.reshape(nx, 1, LANES), "gx", 0, 0, tiled=True, axis_index_groups=order)
    (air,) = call(owner_kernel, "owner", [((2, 1, 256), F32)], 1, 1 << 20)(got.reshape(nx, LANES))
    return temperature, salinity, air


def solution(mesh):
    placed = (
        P(None, "gy", "gx"),
        P(None, "gy", "gx"),
        P(None, "gy", "gx"),
        P(None, "gy", "gx"),
        P("gy", "gx"),
        P(None, "gy", "gx"),
        P("gy", "gx"),
        P("gy", "gx"),
        P("gy", "gx"),
        P("gy", "gx"),
        P(),
        P("gy", None),
    )
    return jax.shard_map(
        shards,
        mesh=mesh,
        in_specs=placed,
        out_specs=(P(None, "gy", "gx"), P(None, "gy", "gx"), P(None, "gy", "gx")),
        check_vma=False,
    )
```
